32 devices in a mesh: dom: 8 (over z, x), blk: 4 (over y, core).
Axes of the slice: x: 2, y: 2, z: 4, core: 2. Of those that a mesh axis runs over, the one named last changes fastest.
Arguments:
- multipliers: float32 [4, 48, 64, 256], P('blk', 'dom'), may hold values from -6 to 6
- residual: float32 [4, 48, 64, 256], P('blk', 'dom')
- dir_prev: float32 [4, 48, 64, 256], P('blk', 'dom'), may hold values from -6 to 6
- rho_prev: float32 [64], replicated, may hold values from 10 to 100
- face_ids: int32 [4, 16, 6], P('blk'), may hold values from 0 to 47, as said below
- face_sign: int32 [4, 16, 6], P('blk'), may hold values from -1 to 1, as said below
- dual_blocks: bfloat16 [4, 16, 1536, 1536], P('blk', 'dom'), as said below
- dirichlet_blocks: bfloat16 [4, 16, 1536, 1536], P('blk', 'dom'), as said below
- coupling: bfloat16 [4, 16, 256, 1536], P('blk', 'dom'), may hold values from -0.15625 to 0.15625
- corner_ids: int32 [4, 16, 256], P('blk', 'dom'), may hold values from 0 to 3071, as said below
- coarse_inv: bfloat16 [8, 4, 768, 768], P('dom', 'blk'), as said below
Outputs:
- new_multipliers: float32 [4, 48, 64, 256], P('blk', 'dom')
- new_residual: float32 [4, 48, 64, 256], P('blk', 'dom')
- direction: float32 [4, 48, 64, 256], P('blk', 'dom')
- rho_now: float32 [64], replicated
- reduction: float32 [64], replicated
The draws below stay inside these ranges and needn't reach their ends.
Inputs may be any that keep to these rules, and one draw needn't show every extreme that they name: `face_ids`: in each column b every face index below 48 is named by exactly two slots, of subdomains held by two different indices of dom; face f is owned by dom index f // 6. The 2 subdomains of one dom index name at most 3 faces of any one owner, and in every column some pairs of a dom index and an owner reach 3. `face_sign`: of the two slots that name one face, one has +1 and the other -1. `dual_blocks`: each block is symmetric positive definite. `dirichlet_blocks`: each block is symmetric positive definite. `coarse_inv`: each block is symmetric positive definite. `corner_ids`: the corners of one subdomain are distinct, and corner k lies in coarse block k // 64, that is, its index n satisfies n // 768 = k // 64.
All inputs are finite; a program needn't handle non-finite values.
Results may differ from the reference program's by a relative error of at most 0.033.
Values may be sent and summed in bfloat16 or wider, within the bound.
A program may use at most 128 MiB of HBM per device.

```python
import math
import jax
import jax.numpy as jnp
from jax import lax

FDOF = 256
CASES = 64
FPS = 6
SUB_DEV = 2
CB = 768
NCD = 256
LOCAL = 1536
FACE_DEV = 6
CAP = 3
NSC = 16
NFC = 48
N_DOM = 8
N_BLK = 4


def face_pattern(key):
    base_key = jax.random.fold_in(key, 5)
    slot_total = FPS * SUB_DEV

    def shuffled(place_key_one):
        return jax.random.permutation(place_key_one, slot_total)

    def column_pattern(column_key):
        perm_key, place_key = jax.random.split(column_key)
        offsets_perm = jax.random.permutation(perm_key, N_DOM)
        element = jnp.arange(slot_total)
        cycle_index = 1 + jnp.maximum(element - CAP, 0) % (N_DOM - 1)
        offsets = jnp.where(element < CAP, offsets_perm[0], offsets_perm[cycle_index])
        dom_rows = jnp.arange(N_DOM)
        owner = (dom_rows[:, None] - offsets[None, :]) % N_DOM
        faces = owner * FACE_DEV + (element % FACE_DEV)[None, :]
        signs = jnp.broadcast_to(jnp.where(element < FACE_DEV, 1, -1)[None, :], (N_DOM, slot_total))
        place_keys = jax.random.split(place_key, N_DOM)
        placement = jax.vmap(shuffled)(place_keys)
        inverse = jnp.argsort(placement, axis=1, stable=True)
        faces = jnp.take_along_axis(faces, inverse, axis=1)
        signs = jnp.take_along_axis(signs, inverse, axis=1)
        return (faces.reshape(N_DOM * SUB_DEV, FPS).astype(jnp.int32), signs.reshape(N_DOM * SUB_DEV, FPS).astype(jnp.int32))
    column_keys = jax.random.split(base_key, N_BLK)
    return jax.vmap(column_pattern)(column_keys)


def draw_face_ids(key, part):
    return face_pattern(key)[0]


def draw_face_sign(key, part):
    return face_pattern(key)[1]


def draw_corner_ids(key, part):
    base_key = jax.random.fold_in(key, 31)
    share = NCD // N_BLK
    count = N_BLK * N_DOM * SUB_DEV * N_BLK
    keys = jax.random.split(base_key, count)

    def one_perm(perm_key):
        return jax.random.permutation(perm_key, CB)[:share]
    picks = jax.vmap(one_perm)(keys).reshape(N_BLK, N_DOM * SUB_DEV, N_BLK, share)
    sub_index = jnp.arange(N_DOM * SUB_DEV)[None, :, None, None]
    block_index = jnp.arange(N_BLK)[None, None, :, None]
    first = picks[:, :, :, :1]
    shift_high = jnp.where((sub_index == 0) & (block_index == N_BLK - 1), CB - 1 - first, 0)
    shift_low = jnp.where((sub_index == 0) & (block_index == 0), -first, 0)
    moved = (picks + shift_high + shift_low) % CB
    ids = moved + block_index * CB
    return ids.reshape(N_BLK, N_DOM * SUB_DEV, NCD).astype(jnp.int32)


def spd_stack(key, leading, matrix_order):
    block_count = leading[0] * leading[1]

    def single_block(block_index):
        block_key = jax.random.fold_in(key, block_index)
        noise_key, diag_key = jax.random.split(block_key)
        noise_vals = jax.random.normal(noise_key, (matrix_order, matrix_order), jnp.float32)
        symmetric = (noise_vals + noise_vals.T) * (0.7 / math.sqrt(2.0 * matrix_order))
        diagonal = jnp.exp(jax.random.uniform(diag_key, (matrix_order,), jnp.float32, math.log(2.2), math.log(4.4)))
        return (symmetric + jnp.diag(diagonal)).astype(jnp.bfloat16)
    blocks = lax.map(single_block, jnp.arange(block_count))
    return blocks.reshape(leading + (matrix_order, matrix_order))


def draw_dual_blocks(key, part):
    return spd_stack(jax.random.fold_in(key, 21), (N_BLK, N_DOM * SUB_DEV), FPS * FDOF)


def draw_dirichlet_blocks(key, part):
    return spd_stack(jax.random.fold_in(key, 22), (N_BLK, N_DOM * SUB_DEV), FPS * FDOF)


def draw_coarse_inv(key, part):
    return spd_stack(jax.random.fold_in(key, 23), (N_DOM, N_BLK), CB)


def draw_residual(key, part):
    noise_key = jax.random.fold_in(key, 11)
    shape = (N_BLK, N_DOM * FACE_DEV, CASES, FDOF)
    owner = (jnp.arange(N_DOM * FACE_DEV) // FACE_DEV).astype(jnp.float32)
    column = jnp.arange(N_BLK).astype(jnp.float32)
    rise = (1.0 + 2.0 * owner / (N_DOM - 1))[None, :, None, None] * (1.0 + 0.5 * column / max(N_BLK - 1, 1))[:, None, None, None]
    base_vals = jax.random.normal(noise_key, shape, jnp.float32)
    return (base_vals * rise).astype(jnp.float32)


def steps_of(rng, extent, shards, least, high):
    gain, own = 1.0, jax.random.fold_in(rng, 6)
    for position, parts in shards:
        steps = jnp.exp(jax.random.uniform(jax.random.fold_in(own, position), (parts,), jnp.float32, least / len(shards), high / len(shards)))
        gain = gain * jnp.repeat(steps, extent[position] // parts).reshape([-1 if axis == position else 1 for axis in range(len(extent))])
    return gain


def noise(stream_key, extent, scale, most, cuts=(), held_as=jnp.bfloat16):
    result = jax.random.normal(stream_key, extent, jnp.float32) * scale
    if len(cuts) > 0:
        result = steps_of(stream_key, extent, cuts, -0.22, 0.18) * result
    return jnp.clip(result, min=-most, max=most).astype(held_as)


def setup_inputs(seed: int = 0) -> dict:
    key_list = jax.random.split(jax.random.key(seed), 12)
    return {
        "multipliers": noise(key_list[0], (N_BLK, NFC, CASES, FDOF), 1.0, 6.0, ((0, 4), (1, 8)), jnp.float32),
        "residual": draw_residual(jax.random.fold_in(key_list[11], 71), 0),
        "dir_prev": noise(key_list[2], (N_BLK, NFC, CASES, FDOF), 1.0, 6.0, ((0, 4), (1, 8)), jnp.float32),
        "rho_prev": jnp.clip(jnp.exp(jax.random.uniform(key_list[3], (CASES,), jnp.float32, math.log(10.0), math.log(100.0))), 10.0, 100.0),
        "face_ids": draw_face_ids(jax.random.fold_in(key_list[11], 71), 0),
        "face_sign": draw_face_sign(jax.random.fold_in(key_list[11], 71), 0),
        "dual_blocks": draw_dual_blocks(jax.random.fold_in(key_list[11], 71), 0),
        "dirichlet_blocks": draw_dirichlet_blocks(jax.random.fold_in(key_list[11], 71), 0),
        "coupling": noise(key_list[8], (N_BLK, NSC, NCD, LOCAL), LOCAL ** -0.5, 0.15625, ((0, 4), (1, 8))),
        "corner_ids": draw_corner_ids(jax.random.fold_in(key_list[11], 71), 0),
        "coarse_inv": draw_coarse_inv(jax.random.fold_in(key_list[11], 71), 0),
    }


def pull_slots(vector, face_ids, face_sign):
    vector_half = vector.astype(jnp.bfloat16)

    def column_pick(column_vec, column_ids):
        return column_vec[column_ids]

    picked = jax.vmap(column_pick)(vector_half, face_ids)
    return picked * face_sign.astype(jnp.bfloat16)[:, :, :, None, None]


def local_products(slots, matrices):
    def column_product(operands):
        pieces, blocks = operands
        wide = blocks.astype(jnp.float32).reshape(N_DOM * SUB_DEV, FPS, FDOF, FPS * FDOF)
        return jnp.einsum("stcx,stxm->scm", pieces.astype(jnp.float32), wide)

    return lax.map(column_product, (slots, matrices))


def push_faces(totals, face_ids, face_sign):
    per_slot = totals.reshape(N_BLK, N_DOM * SUB_DEV, CASES, FPS, FDOF)
    per_slot = per_slot * face_sign.astype(jnp.float32)[:, :, None, :, None]
    rounded = lax.optimization_barrier(per_slot.astype(jnp.bfloat16)).astype(jnp.float32)
    rounded = jnp.transpose(rounded, (0, 1, 3, 2, 4)).reshape(N_BLK, N_DOM * SUB_DEV * FPS, CASES, FDOF)

    def column_add(column_ids, column_vals):
        start_sums = jnp.zeros((N_DOM * FACE_DEV, CASES, FDOF), jnp.float32)
        return start_sums.at[column_ids.reshape(-1)].add(column_vals)

    return jax.vmap(column_add)(face_ids, rounded)


def coarse_term(slots, coupling, corner_ids, coarse_inv):
    wide = coupling.astype(jnp.float32).reshape(N_BLK, N_DOM * SUB_DEV, NCD, FPS, FDOF)
    corner_terms = jnp.einsum("bjtcx,bjktx->bjck", slots.astype(jnp.float32), wide)
    corner_terms = corner_terms.reshape(N_BLK, N_DOM, SUB_DEV, CASES, NCD)
    index_rows = corner_ids.reshape(N_BLK, N_DOM, SUB_DEV, NCD)

    def column_assemble(column_terms, column_index):
        values = jnp.transpose(column_terms, (2, 0, 1, 3)).reshape(CASES, N_BLK * SUB_DEV * NCD)
        start_sums = jnp.zeros((CASES, N_BLK * CB), jnp.float32)
        return start_sums.at[:, column_index.reshape(-1)].add(values)

    coarse_rhs = jax.vmap(column_assemble, in_axes=(1, 1))(corner_terms, index_rows)
    coarse_half = lax.optimization_barrier(coarse_rhs.astype(jnp.bfloat16))
    coarse_half = coarse_half.astype(jnp.float32).reshape(N_DOM, CASES, N_BLK, CB)
    solved = jnp.einsum("dcbm,dbmn->dcbn", coarse_half, coarse_inv.astype(jnp.float32))
    solved = lax.optimization_barrier(solved.astype(jnp.bfloat16))
    solved = solved.astype(jnp.float32).reshape(N_DOM, CASES, N_BLK * CB)

    def column_pick(column_sol, column_index):
        return column_sol[:, column_index]

    picked = jax.vmap(column_pick, in_axes=(0, 1))(solved, index_rows)
    picked = jnp.transpose(picked, (2, 0, 3, 1, 4)).reshape(N_BLK, N_DOM * SUB_DEV, CASES, NCD)
    return jnp.einsum("bjck,bjkl->bjcl", picked, coupling.astype(jnp.float32))


def reference(multipliers, residual, dir_prev, rho_prev, face_ids, face_sign, dual_blocks, dirichlet_blocks, coupling, corner_ids, coarse_inv):
    total_count = N_BLK * N_DOM * FACE_DEV * FDOF
    slots = pull_slots(residual, face_ids, face_sign)
    precond_res = push_faces(local_products(slots, dirichlet_blocks), face_ids, face_sign)
    rho_now = jnp.sum(residual * precond_res, axis=(0, 1, 3)) / total_count
    res_mean = jnp.sum(residual * residual, axis=(0, 1, 3)) / total_count
    beta_ratio = rho_now / rho_prev
    direction = precond_res + beta_ratio[None, None, :, None] * dir_prev
    slots = pull_slots(direction, face_ids, face_sign)
    totals = local_products(slots, dual_blocks) + coarse_term(slots, coupling, corner_ids, coarse_inv)
    image = push_faces(totals, face_ids, face_sign)
    curvature = jnp.sum(direction * image, axis=(0, 1, 3)) / total_count
    alpha_step = rho_now / curvature
    new_multipliers = multipliers + alpha_step[None, None, :, None] * direction
    new_residual = residual - alpha_step[None, None, :, None] * image
    reduction = (jnp.sum(new_residual * new_residual, axis=(0, 1, 3)) / total_count) / res_mean
    return new_multipliers, new_residual, direction, rho_now, reduction
```

```python
import jax
import jax.numpy as jnp
from jax import lax
from jax.experimental import pallas as pl
from jax.experimental.pallas import tpu as pltpu
from jax.sharding import PartitionSpec as P

MESH = pl.DeviceIdType.MESH
F32, BF16 = jnp.float32, jnp.bfloat16
ROWS, LANES = 16, 128


def remote(src, dst, send, recv, axis, peer):
    return pltpu.make_async_remote_copy(
        src_ref=src, dst_ref=dst, send_sem=send, recv_sem=recv,
        device_id={axis: peer}, device_id_type=MESH,
    )


def lane_sum(value):
    return jnp.sum(value, axis=1, keepdims=True)


def as_column(row, cases):
    tile = jnp.concatenate([row, jnp.zeros((127, row.shape[1]), F32)], axis=0)
    return jnp.transpose(tile)[:cases, :1]


def columns_tile(columns):
    rows = columns[0].shape[0]
    place = lax.broadcasted_iota(jnp.int32, (rows, 128), 1)
    tile = jnp.zeros((rows, 128), F32)
    for i, column in enumerate(columns):
        tile = jnp.where(place == i, column, tile)
    return tile


def step_kernel(
    face_ids, face_sign, first, second,
    res_hbm, dir_hbm, rho_ref, ids_ref,
    dirichlet, dual, coupling, inverse,
    image_in, precond_in, stats,
    w_dir, w_dual, w_cpl, w_inv, res, dirp,
    res_out, res_in, dir_out, dir_in,
    slot_out, slot_in, push_out, push_in, precond_out, image_out,
    sums, direction, chosen, slots, products, square,
    part, dom_sums, blk_sums, wide, hot, ids,
    terms_out, terms_in, picks_out, picks_in,
    load, send_x, recv_x, send_s, recv_s, send_t, recv_t,
):
    n_dom, n_blk = lax.axis_size("dom"), lax.axis_size("blk")
    me, my_blk = lax.axis_index("dom"), lax.axis_index("blk")
    faces, cases, face_len = res.shape
    subs = slots.shape[1]
    local = slots.shape[3]
    fps = local // face_len
    slot_count = subs * fps
    halves = face_len // LANES
    relays = (cases // ROWS) * halves
    group = (me // relays) * relays
    my_chunk = lax.rem(me, relays)
    my_rows = pl.multiple_of((my_chunk // halves) * ROWS, ROWS)
    count = n_dom * n_blk * faces * face_len
    share = ids.shape[2]
    span = w_inv.shape[0]
    all_peers = [(k - 1, lax.rem(me + k, n_dom)) for k in range(1, n_dom)]
    group_peers = [(k - 1, group + lax.rem(my_chunk + k, relays)) for k in range(1, relays)]
    blk_peers = [(k - 1, lax.rem(my_blk + k, n_blk)) for k in range(1, n_blk)]

    loads = [
        pltpu.make_async_copy(src, dst, load.at[i])
        for i, (src, dst) in enumerate((
            (res_hbm, res), (dirichlet, w_dir), (dir_hbm, dirp),
            (coupling, w_cpl), (dual, w_dual), (inverse, w_inv),
        ))
    ]
    for copy in loads:
        copy.start()

    barrier = pltpu.get_barrier_semaphore()
    for axis, peers in (("dom", all_peers), ("blk", blk_peers)):
        for _, peer in peers:
            pl.semaphore_signal(barrier, inc=1, device_id={axis: peer}, device_id_type=MESH)

    def chunk_of(k):
        q, h = k // halves, k % halves
        return slice(q * ROWS, (q + 1) * ROWS), slice(h * LANES, (h + 1) * LANES)

    def start(copies):
        for copy in copies:
            copy.start()
        return copies

    def finish(copies):
        for copy in copies:
            copy.wait()

    def to_relays(turn, out, into):
        width = out.shape[1]
        copies = start([
            remote(
                out.at[lax.rem(peer, relays)], into.at[pl.ds(me * width, width)],
                send_x.at[turn, k], recv_x.at[turn, k], "dom", peer,
            )
            for k, peer in all_peers
        ])
        own = out[my_chunk]
        into[pl.ds(me * width, width)] = own
        return copies

    def to_group(turn, source, into):
        copies = start([
            remote(
                source(peer), into.at[my_chunk],
                send_x.at[turn, k], recv_x.at[turn, k], "dom", peer,
            )
            for k, peer in group_peers
        ])
        into[my_chunk] = source(me)[...]
        return copies

    def face_of(d, s):
        return face_ids[s % fps, 0, d * subs + s // fps]

    def sign_of(s):
        return face_sign[s % fps, 0, me * subs + s // fps].astype(F32)

    def split(field, out):
        for f in range(faces):
            value = field[f].astype(BF16)
            for k in range(relays):
                rows, lanes = chunk_of(k)
                out[k, f] = value[rows, lanes]

    def hand_out(turn, held):
        for i in range(relays):
            for s in range(slot_count):
                slot_out[turn, i, s] = held[face_of(group + i, s)]

    def to_slots(turn):
        for s in range(slot_count):
            sub, t = divmod(s, fps)
            sign = sign_of(s)
            for k in range(relays):
                rows, lanes = chunk_of(k)
                value = slot_in[turn, k, s].astype(F32) * sign
                slots[turn, sub, rows, t * face_len + lanes.start:t * face_len + lanes.stop] = value.astype(BF16)

    def product(turn, weights, sub, t):
        return jnp.dot(
            slots[turn, sub], weights[sub, :, t * face_len:(t + 1) * face_len],
            preferred_element_type=F32,
        )

    def put(turn, s, value):
        for k in range(relays):
            rows, lanes = chunk_of(k)
            push_out[turn, k, s] = value[rows, lanes]

    def reduce_start(turn, tile, axis, peers, into, base):
        part[turn] = tile
        here = lax.axis_index(axis)
        copies = start([
            remote(
                part.at[turn], into.at[here], send_s.at[turn, k], recv_s.at[turn, k], axis, peer
            )
            for k, peer in peers
        ])
        into[here] = tile
        return copies

    def reduce_end(copies, into, base, number):
        finish(copies)
        total = into[base]
        for i in range(1, number):
            total = total + into[base + i]
        return total

    loads[0].wait()
    split(res, res_out)
    pl.semaphore_wait(barrier, n_dom + n_blk - 2)
    pulled = to_relays(0, res_out, res_in)

    for b in range(n_blk):
        ids[n_blk + b, :subs] = ids_ref[:, b * share:(b + 1) * share] - b * span
    id_copies = start([
        remote(
            ids.at[n_blk + peer], ids.at[my_blk], send_t.at[2, k], recv_t.at[2, k], "blk", peer
        )
        for k, peer in blk_peers
    ])
    ids[my_blk] = ids[n_blk + my_blk]
    total = jnp.zeros((cases, face_len), F32)
    for f in range(faces):
        total += res[f] * res[f]
    square[...] = jnp.broadcast_to(lane_sum(total), (cases, 128))
    loads[2].wait()
    split(dirp, dir_out)

    finish(pulled)
    hand_out(0, res_in)
    handed = to_group(1, lambda peer: slot_out.at[0, lax.rem(peer, relays)], slot_in.at[0])
    dir_copies = to_relays(2, dir_out, dir_in)
    finish(id_copies)
    for p in range(n_blk):
        for s in range(subs):
            rows = lax.broadcasted_iota(jnp.int32, (span, share), 0)
            hot[p, s] = (rows == ids[p, s:s + 1, :]).astype(F32).astype(BF16)
    loads[1].wait()
    finish(handed)
    to_slots(0)

    rho_part = jnp.zeros((cases, face_len), F32)
    for s in range(slot_count):
        sub, t = divmod(s, fps)
        value = product(0, w_dir, sub, t)
        sent = (value * sign_of(s)).astype(BF16)
        put(0, s, sent)
        rho_part += (
            slots[0, sub, :, t * face_len:(t + 1) * face_len].astype(F32)
            * value.astype(BF16).astype(F32)
        )
    tile = columns_tile((lane_sum(rho_part), square[:, :1]))
    tile = jnp.transpose(jnp.concatenate([tile, jnp.zeros((128 - cases, 128), F32)], axis=0))[:8]
    rho_copies = reduce_start(0, tile, "dom", all_peers, dom_sums.at[0], 0)
    pushed = to_relays(3, push_out.at[0], push_in.at[0])
    tile = reduce_end(rho_copies, dom_sums.at[0], 0, n_dom)
    rho_copies = reduce_start(1, tile, "blk", blk_peers, blk_sums.at[0], 0)
    tile = reduce_end(rho_copies, blk_sums.at[0], 0, n_blk)
    rho_now = tile[0:1] / count
    square_sum = tile[1:2]
    pad = jnp.ones((1, 128 - cases), F32)
    beta_row = rho_now / jnp.concatenate([rho_ref[...].reshape(1, cases), pad], axis=1)
    wide[:cases] = jnp.broadcast_to(as_column(beta_row, cases), (cases, 128))
    beta = wide[pl.ds(my_rows, ROWS), :]
    finish(dir_copies)
    finish(pushed)
    for f in range(n_dom * faces):
        value = push_in[0, first[f]].astype(F32) + push_in[0, second[f]].astype(F32)
        precond_out[f] = value.astype(BF16)
        value = value + beta * dir_in[f].astype(F32)
        direction[f] = value
        chosen[f] = value.astype(BF16)
    hand_out(1, chosen)
    handed = to_group(4, lambda peer: slot_out.at[1, lax.rem(peer, relays)], slot_in.at[1])
    to_owners = to_group(5, lambda peer: precond_out.at[pl.ds(peer * faces, faces)], precond_in)
    for i in (3, 4, 5):
        loads[i].wait()
    finish(handed)
    to_slots(1)

    for b in range(n_blk):
        for s in range(subs):
            terms_out[b, s] = lax.dot_general(
                slots[1, s], w_cpl[s, b * share:(b + 1) * share, :], (((1,), (1,)), ((), ())),
                preferred_element_type=F32,
            ).astype(BF16)
    copies = start([
        remote(terms_out.at[peer], terms_in.at[my_blk], send_t.at[0, k], recv_t.at[0, k], "blk", peer)
        for k, peer in blk_peers
    ])
    terms_in[my_blk] = terms_out[my_blk]
    for s in range(slot_count):
        sub, t = divmod(s, fps)
        products[s] = product(1, w_dual, sub, t)
    finish(copies)
    rhs = jnp.zeros((cases, span), F32)
    for p in range(n_blk):
        for s in range(subs):
            rhs += lax.dot_general(
                terms_in[p, s], hot[p, s], (((1,), (1,)), ((), ())), preferred_element_type=F32
            )
    solved = jnp.dot(rhs.astype(BF16), w_inv[...], preferred_element_type=F32).astype(BF16)
    for p in range(n_blk):
        for s in range(subs):
            picks_out[p, s] = jnp.dot(solved, hot[p, s], preferred_element_type=F32).astype(BF16)
    copies = start([
        remote(picks_out.at[peer], picks_in.at[my_blk], send_t.at[1, k], recv_t.at[1, k], "blk", peer)
        for k, peer in blk_peers
    ])
    picks_in[my_blk] = picks_out[my_blk]
    finish(copies)
    for s in range(slot_count):
        sub, t = divmod(s, fps)
        value = products[s]
        for b in range(n_blk):
            value += jnp.dot(
                picks_in[b, sub],
                w_cpl[sub, b * share:(b + 1) * share, t * face_len:(t + 1) * face_len],
                preferred_element_type=F32,
            )
        put(1, s, (value * sign_of(s)).astype(BF16))
    pushed = to_relays(6, push_out.at[1], push_in.at[1])
    wide[...] = jnp.zeros((128, 128), F32)
    finish(to_owners)
    finish(pushed)
    curve = jnp.zeros((ROWS, LANES), F32)
    cross = jnp.zeros((ROWS, LANES), F32)
    norm = jnp.zeros((ROWS, LANES), F32)
    for f in range(n_dom * faces):
        value = push_in[1, first[f]].astype(F32) + push_in[1, second[f]].astype(F32)
        image_out[f] = value.astype(BF16)
        curve += direction[f] * value
        cross += res_in[f].astype(F32) * value
        norm += value * value
    wide[pl.ds(my_rows, ROWS), :] = columns_tile((lane_sum(curve), lane_sum(cross), lane_sum(norm)))
    tile = jnp.transpose(wide[...])[:8]
    copies = reduce_start(2, tile, "blk", blk_peers, blk_sums.at[1], 0)
    to_owners = to_group(7, lambda peer: image_out.at[pl.ds(peer * faces, faces)], image_in)
    tile = reduce_end(copies, blk_sums.at[1], 0, n_blk)
    copies = reduce_start(3, tile, "dom", group_peers, dom_sums.at[1], 0)
    tile = reduce_end(copies, dom_sums.at[1], group, relays)
    alpha = rho_now / (tile[0:1] / count)
    new_sum = square_sum - 2.0 * alpha * tile[1:2] + alpha * alpha * tile[2:3]
    stats[0:1] = rho_now
    stats[1:2] = (new_sum / count) / (square_sum / count)
    stats[2:3] = alpha
    stats[3:4] = beta_row
    stats[4:8] = jnp.zeros((4, 128), F32)
    finish(to_owners)


def finish_kernel(
    lam, res, dirp, precond, image, stats, new_lam, new_res, new_dir, rho_now, reduction
):
    faces, cases, face_len = lam.shape
    halves = face_len // LANES
    table = stats[...]
    alpha = as_column(table[2:3], cases)
    beta = as_column(table[3:4], cases)
    for k in range(precond.shape[0]):
        rows = slice((k // halves) * ROWS, (k // halves + 1) * ROWS)
        lanes = slice((k % halves) * LANES, (k % halves + 1) * LANES)
        for f in range(faces):
            direction = precond[k, f].astype(F32) + beta[rows] * dirp[f, rows, lanes]
            new_dir[f, rows, lanes] = direction
            new_lam[f, rows, lanes] = lam[f, rows, lanes] + alpha[rows] * direction
            new_res[f, rows, lanes] = res[f, rows, lanes] - alpha[rows] * image[k, f].astype(F32)
    rho_now[...] = table[0:1, :cases].reshape(cases)
    reduction[...] = table[1:2, :cases].reshape(cases)


def on_device(
    multipliers, residual, dir_prev, rho_prev, face_ids, face_sign,
    dual_blocks, dirichlet_blocks, coupling, corner_ids, coarse_inv,
):
    n_dom, n_blk = lax.axis_size("dom"), lax.axis_size("blk")
    _, faces, cases, face_len = multipliers.shape
    _, subs, local, _ = dual_blocks.shape
    fps = face_ids.shape[2]
    slot_count = subs * fps
    relays = (cases // ROWS) * (face_len // LANES)
    total = n_dom * faces
    ids = jnp.transpose(face_ids, (2, 0, 1))
    signs = jnp.transpose(face_sign, (2, 0, 1))
    code = jnp.arange(n_dom * subs)[None, None, :] * fps + jnp.arange(fps)[:, None, None]
    match = ids[None] == jnp.arange(total)[:, None, None, None]
    first = jnp.min(jnp.where(match, code[None], n_dom * slot_count - 1), axis=(1, 2, 3))
    second = jnp.max(jnp.where(match, code[None], 0), axis=(1, 2, 3))
    span = coarse_inv.shape[2]
    corners = coupling.shape[2]
    share = corners // n_blk
    field = jax.ShapeDtypeStruct((faces, cases, face_len), F32)
    vmem = pl.BlockSpec(memory_space=pltpu.VMEM)
    smem = pl.BlockSpec(memory_space=pltpu.SMEM)
    hbm = pl.BlockSpec(memory_space=pl.ANY)
    dma = pltpu.SemaphoreType.DMA
    terms = pltpu.VMEM((n_blk, subs, cases, share), BF16)
    chunk = (ROWS, LANES)
    owned = jax.ShapeDtypeStruct((relays, faces) + chunk, BF16)
    image, precond, stats = pl.pallas_call(
        step_kernel,
        out_shape=(owned, owned, jax.ShapeDtypeStruct((8, 128), F32)),
        in_specs=[smem] * 4 + [hbm] * 2 + [vmem] * 2 + [hbm] * 4,
        out_specs=(vmem,) * 3,
        scratch_shapes=[
            pltpu.VMEM((subs, local, local), BF16),
            pltpu.VMEM((subs, local, local), BF16),
            pltpu.VMEM((subs, corners, local), BF16),
            pltpu.VMEM((span, span), BF16),
            pltpu.VMEM((faces, cases, face_len), F32),
            pltpu.VMEM((faces, cases, face_len), F32),
            pltpu.VMEM((relays, faces) + chunk, BF16),
            pltpu.VMEM((total,) + chunk, BF16),
            pltpu.VMEM((relays, faces) + chunk, BF16),
            pltpu.VMEM((total,) + chunk, BF16),
            pltpu.VMEM((2, relays, slot_count) + chunk, BF16),
            pltpu.VMEM((2, relays, slot_count) + chunk, BF16),
            pltpu.VMEM((2, relays, slot_count) + chunk, BF16),
            pltpu.VMEM((2, n_dom * slot_count) + chunk, BF16),
            pltpu.VMEM((total,) + chunk, BF16),
            pltpu.VMEM((total,) + chunk, BF16),
            pltpu.VMEM((total,) + chunk, F32),
            pltpu.VMEM((total,) + chunk, F32),
            pltpu.VMEM((total,) + chunk, BF16),
            pltpu.VMEM((2, subs, cases, local), BF16),
            pltpu.VMEM((slot_count, cases, face_len), F32),
            pltpu.VMEM((cases, 128), F32),
            pltpu.VMEM((4, 8, 128), F32),
            pltpu.VMEM((2, n_dom, 8, 128), F32),
            pltpu.VMEM((2, n_blk, 8, 128), F32),
            pltpu.VMEM((128, 128), F32),
            pltpu.VMEM((n_blk, subs, span, share), BF16),
            pltpu.VMEM((2 * n_blk, 8, share), jnp.int32),
            terms, terms, terms, terms,
            dma((6,)),
            dma((8, n_dom - 1)), dma((8, n_dom - 1)),
            dma((4, max(n_dom, n_blk) - 1)), dma((4, max(n_dom, n_blk) - 1)),
            dma((3, n_blk - 1)), dma((3, n_blk - 1)),
        ],
        compiler_params=pltpu.CompilerParams(
            collective_id=0, has_side_effects=True, vmem_limit_bytes=60 << 20
        ),
    )(
        ids, signs, first, second,
        residual[0], dir_prev[0], rho_prev, corner_ids[0],
        dirichlet_blocks[0], dual_blocks[0], coupling[0], coarse_inv[0, 0],
    )
    row = jax.ShapeDtypeStruct((cases,), F32)
    new_lam, new_res, new_dir, rho_now, reduction = pl.pallas_call(
        finish_kernel,
        out_shape=(field, field, field, row, row),
        in_specs=[vmem] * 6,
        out_specs=(vmem,) * 5,
    )(multipliers[0], residual[0], dir_prev[0], precond, image, stats)
    return new_lam[None], new_res[None], new_dir[None], rho_now, reduction


def solution(mesh):
    in_specs = (
        P("blk", "dom", None, None),
        P("blk", "dom", None, None),
        P("blk", "dom", None, None),
        P(),
        P("blk", None, None),
        P("blk", None, None),
        P("blk", "dom", None, None),
        P("blk", "dom", None, None),
        P("blk", "dom", None, None),
        P("blk", "dom", None),
        P("dom", "blk", None, None),
    )
    out_specs = (
        P("blk", "dom", None, None),
        P("blk", "dom", None, None),
        P("blk", "dom", None, None),
        P(),
        P(),
    )
    return jax.shard_map(
        on_device, mesh=mesh, in_specs=in_specs, out_specs=out_specs, check_vma=False
    )
```

```python
import jax
import jax.numpy as jnp
from jax import lax
from jax.experimental import pallas as pl
from jax.experimental.pallas import tpu as pltpu
from jax.sharding import PartitionSpec as P

MESH = pl.DeviceIdType.MESH
F32, BF16 = jnp.float32, jnp.bfloat16
ROWS, LANES = 16, 128


def remote(src, dst, send, recv, axis, peer):
    return pltpu.make_async_remote_copy(
        src_ref=src, dst_ref=dst, send_sem=send, recv_sem=recv,
        device_id={axis: peer}, device_id_type=MESH,
    )


def lane_sum(value):
    return jnp.sum(value, axis=1, keepdims=True)


def as_column(row, cases):
    tile = jnp.concatenate([row, jnp.zeros((127, row.shape[1]), F32)], axis=0)
    return jnp.transpose(tile)[:cases, :1]


def columns_tile(columns):
    rows = columns[0].shape[0]
    place = lax.broadcasted_iota(jnp.int32, (rows, 128), 1)
    tile = jnp.zeros((rows, 128), F32)
    for i, column in enumerate(columns):
        tile = jnp.where(place == i, column, tile)
    return tile


def step_kernel(
    face_ids, face_sign, first, second,
    res_hbm, dir_hbm, rho_ref, ids_ref,
    dirichlet, dual, coupling, inverse,
    image_in, precond_in, stats,
    w_dir, w_dual, w_cpl, w_inv, res, dirp,
    res_out, res_in, dir_out, dir_in,
    slot_out, slot_in, push_out, push_in, precond_out, image_out,
    sums, direction, chosen, slots, products, square,
    part, dom_sums, blk_sums, wide, hot, ids,
    terms_out, terms_in, picks_out, picks_in,
    load, send_x, recv_x, send_s, recv_s, send_t, recv_t,
):
    n_dom, n_blk = lax.axis_size("dom"), lax.axis_size("blk")
    me, my_blk = lax.axis_index("dom"), lax.axis_index("blk")
    faces, cases, face_len = res.shape
    subs = slots.shape[1]
    local = slots.shape[3]
    fps = local // face_len
    slot_count = subs * fps
    halves = face_len // LANES
    relays = (cases // ROWS) * halves
    group = (me // relays) * relays
    my_chunk = lax.rem(me, relays)
    my_rows = pl.multiple_of((my_chunk // halves) * ROWS, ROWS)
    count = n_dom * n_blk * faces * face_len
    share = ids.shape[2]
    span = w_inv.shape[0]
    all_peers = [(k - 1, lax.rem(me + k, n_dom)) for k in range(1, n_dom)]
    group_peers = [(k - 1, group + lax.rem(my_chunk + k, relays)) for k in range(1, relays)]
    blk_peers = [(k - 1, lax.rem(my_blk + k, n_blk)) for k in range(1, n_blk)]

    loads = [
        pltpu.make_async_copy(src, dst, load.at[i])
        for i, (src, dst) in enumerate((
            (res_hbm, res), (dirichlet, w_dir), (dir_hbm, dirp),
            (coupling, w_cpl), (dual, w_dual), (inverse, w_inv),
        ))
    ]
    for copy in loads:
        copy.start()

    barrier = pltpu.get_barrier_semaphore()
    for axis, peers in (("dom", all_peers), ("blk", blk_peers)):
        for _, peer in peers:
            pl.semaphore_signal(barrier, inc=1, device_id={axis: peer}, device_id_type=MESH)

    def chunk_of(k):
        q, h = k // halves, k % halves
        return slice(q * ROWS, (q + 1) * ROWS), slice(h * LANES, (h + 1) * LANES)

    def start(copies):
        for copy in copies:
            copy.start()
        return copies

    def finish(copies):
        for copy in copies:
            copy.wait()

    def to_relays(turn, out, into):
        width = out.shape[1]
        copies = start([
            remote(
                out.at[lax.rem(peer, relays)], into.at[pl.ds(me * width, width)],
                send_x.at[turn, k], recv_x.at[turn, k], "dom", peer,
            )
            for k, peer in all_peers
        ])
        own = out[my_chunk]
        into[pl.ds(me * width, width)] = own
        return copies

    def to_group(turn, source, into):
        copies = start([
            remote(
                source(peer), into.at[my_chunk],
                send_x.at[turn, k], recv_x.at[turn, k], "dom", peer,
            )
            for k, peer in group_peers
        ])
        into[my_chunk] = source(me)[...]
        return copies

    def face_of(d, s):
        return face_ids[s % fps, 0, d * subs + s // fps]

    def sign_of(s):
        return face_sign[s % fps, 0, me * subs + s // fps].astype(F32)

    def split(field, out):
        for f in range(faces):
            value = field[f].astype(BF16)
            for k in range(relays):
                rows, lanes = chunk_of(k)
                out[k, f] = value[rows, lanes]

    def hand_out(turn, held):
        for i in range(relays):
            for s in range(slot_count):
                slot_out[turn, i, s] = held[face_of(group + i, s)]

    def to_slots(turn):
        for s in range(slot_count):
            sub, t = divmod(s, fps)
            sign = sign_of(s)
            for k in range(relays):
                rows, lanes = chunk_of(k)
                value = slot_in[turn, k, s].astype(F32) * sign
                slots[turn, sub, rows, t * face_len + lanes.start:t * face_len + lanes.stop] = value.astype(BF16)

    def product(turn, weights, sub, t):
        return jnp.dot(
            slots[turn, sub], weights[sub, :, t * face_len:(t + 1) * face_len],
            preferred_element_type=F32,
        )

    def put(turn, s, value):
        for k in range(relays):
            rows, lanes = chunk_of(k)
            push_out[turn, k, s] = value[rows, lanes]

    def reduce_start(turn, tile, axis, peers, into, base):
        part[turn] = tile
        here = lax.axis_index(axis)
        copies = start([
            remote(
                part.at[turn], into.at[here], send_s.at[turn, k], recv_s.at[turn, k], axis, peer
            )
            for k, peer in peers
        ])
        into[here] = tile
        return copies

    def reduce_end(copies, into, base, number):
        finish(copies)
        total = into[base]
        for i in range(1, number):
            total = total + into[base + i]
        return total

    loads[0].wait()
    split(res, res_out)
    pl.semaphore_wait(barrier, n_dom + n_blk - 2)
    pulled = to_relays(0, res_out, res_in)

    for b in range(n_blk):
        ids[n_blk + b, :subs] = ids_ref[:, b * share:(b + 1) * share] - b * span
    id_copies = start([
        remote(
            ids.at[n_blk + peer], ids.at[my_blk], send_t.at[2, k], recv_t.at[2, k], "blk", peer
        )
        for k, peer in blk_peers
    ])
    ids[my_blk] = ids[n_blk + my_blk]
    total = jnp.zeros((cases, face_len), F32)
    for f in range(faces):
        total += res[f] * res[f]
    square[...] = jnp.broadcast_to(lane_sum(total), (cases, 128))
    loads[2].wait()
    split(dirp, dir_out)

    finish(pulled)
    hand_out(0, res_in)
    handed = to_group(1, lambda peer: slot_out.at[0, lax.rem(peer, relays)], slot_in.at[0])
    dir_copies = to_relays(2, dir_out, dir_in)
    finish(id_copies)
    for p in range(n_blk):
        for s in range(subs):
            rows = lax.broadcasted_iota(jnp.int32, (span, share), 0)
            hot[p, s] = (rows == ids[p, s:s + 1, :]).astype(F32).astype(BF16)
    loads[1].wait()
    finish(handed)
    to_slots(0)

    rho_part = jnp.zeros((cases, face_len), F32)
    for s in range(slot_count):
        sub, t = divmod(s, fps)
        value = product(0, w_dir, sub, t)
        sent = (value * sign_of(s)).astype(BF16)
        put(0, s, sent)
        rho_part += (
            slots[0, sub, :, t * face_len:(t + 1) * face_len].astype(F32)
            * value.astype(BF16).astype(F32)
        )
    tile = columns_tile((lane_sum(rho_part), square[:, :1]))
    tile = jnp.transpose(jnp.concatenate([tile, jnp.zeros((128 - cases, 128), F32)], axis=0))[:8]
    rho_copies = reduce_start(0, tile, "dom", all_peers, dom_sums.at[0], 0)
    pushed = to_relays(3, push_out.at[0], push_in.at[0])
    tile = reduce_end(rho_copies, dom_sums.at[0], 0, n_dom)
    rho_copies = reduce_start(1, tile, "blk", blk_peers, blk_sums.at[0], 0)
    tile = reduce_end(rho_copies, blk_sums.at[0], 0, n_blk)
    rho_now = tile[0:1] / count
    square_sum = tile[1:2]
    pad = jnp.ones((1, 128 - cases), F32)
    beta_row = rho_now / jnp.concatenate([rho_ref[...].reshape(1, cases), pad], axis=1)
    wide[:cases] = jnp.broadcast_to(as_column(beta_row, cases), (cases, 128))
    beta = wide[pl.ds(my_rows, ROWS), :]
    finish(dir_copies)
    finish(pushed)
    for f in range(n_dom * faces):
        value = push_in[0, first[f]].astype(F32) + push_in[0, second[f]].astype(F32)
        precond_out[f] = value.astype(BF16)
        value = value + beta * dir_in[f].astype(F32)
        direction[f] = value
        chosen[f] = value.astype(BF16)
    hand_out(1, chosen)
    handed = to_group(4, lambda peer: slot_out.at[1, lax.rem(peer, relays)], slot_in.at[1])
    to_owners = to_group(5, lambda peer: precond_out.at[pl.ds(peer * faces, faces)], precond_in)
    for i in (3, 4, 5):
        loads[i].wait()
    finish(handed)
    to_slots(1)

    for b in range(n_blk):
        for s in range(subs):
            terms_out[b, s] = lax.dot_general(
                slots[1, s], w_cpl[s, b * share:(b + 1) * share, :], (((1,), (1,)), ((), ())),
                preferred_element_type=F32,
            ).astype(BF16)
    copies = start([
        remote(terms_out.at[peer], terms_in.at[my_blk], send_t.at[0, k], recv_t.at[0, k], "blk", peer)
        for k, peer in blk_peers
    ])
    terms_in[my_blk] = terms_out[my_blk]
    for s in range(slot_count):
        sub, t = divmod(s, fps)
        products[s] = product(1, w_dual, sub, t)
    finish(copies)
    rhs = jnp.zeros((cases, span), F32)
    for p in range(n_blk):
        for s in range(subs):
            rhs += lax.dot_general(
                terms_in[p, s], hot[p, s], (((1,), (1,)), ((), ())), preferred_element_type=F32
            )
    solved = jnp.dot(rhs.astype(BF16), w_inv[...], preferred_element_type=F32).astype(BF16)
    for p in range(n_blk):
        for s in range(subs):
            picks_out[p, s] = jnp.dot(solved, hot[p, s], preferred_element_type=F32).astype(BF16)
    copies = start([
        remote(picks_out.at[peer], picks_in.at[my_blk], send_t.at[1, k], recv_t.at[1, k], "blk", peer)
        for k, peer in blk_peers
    ])
    picks_in[my_blk] = picks_out[my_blk]
    finish(copies)
    for s in range(slot_count):
        sub, t = divmod(s, fps)
        value = products[s]
        for b in range(n_blk):
            value += jnp.dot(
                picks_in[b, sub],
                w_cpl[sub, b * share:(b + 1) * share, t * face_len:(t + 1) * face_len],
                preferred_element_type=F32,
            )
        put(1, s, (value * sign_of(s)).astype(BF16))
    pushed = to_relays(6, push_out.at[1], push_in.at[1])
    wide[...] = jnp.zeros((128, 128), F32)
    finish(to_owners)
    finish(pushed)
    curve = jnp.zeros((ROWS, LANES), F32)
    cross = jnp.zeros((ROWS, LANES), F32)
    norm = jnp.zeros((ROWS, LANES), F32)
    for f in range(n_dom * faces):
        value = push_in[1, first[f]].astype(F32) + push_in[1, second[f]].astype(F32)
        image_out[f] = value.astype(BF16)
        curve += direction[f] * value
        cross += res_in[f].astype(F32) * value
        norm += value * value
    wide[pl.ds(my_rows, ROWS), :] = columns_tile((lane_sum(curve), lane_sum(cross), lane_sum(norm)))
    tile = jnp.transpose(wide[...])[:8]
    copies = reduce_start(2, tile, "dom", group_peers, dom_sums.at[1], 0)
    to_owners = to_group(7, lambda peer: image_out.at[pl.ds(peer * faces, faces)], image_in)
    tile = reduce_end(copies, dom_sums.at[1], group, relays)
    copies = reduce_start(3, tile, "blk", blk_peers, blk_sums.at[1], 0)
    tile = reduce_end(copies, blk_sums.at[1], 0, n_blk)
    alpha = rho_now / (tile[0:1] / count)
    new_sum = square_sum - 2.0 * alpha * tile[1:2] + alpha * alpha * tile[2:3]
    stats[0:1] = rho_now
    stats[1:2] = (new_sum / count) / (square_sum / count)
    stats[2:3] = alpha
    stats[3:4] = beta_row
    stats[4:8] = jnp.zeros((4, 128), F32)
    finish(to_owners)


def finish_kernel(
    lam, res, dirp, precond, image, stats, new_lam, new_res, new_dir, rho_now, reduction
):
    faces, cases, face_len = lam.shape
    halves = face_len // LANES
    table = stats[...]
    alpha = as_column(table[2:3], cases)
    beta = as_column(table[3:4], cases)
    for k in range(precond.shape[0]):
        rows = slice((k // halves) * ROWS, (k // halves + 1) * ROWS)
        lanes = slice((k % halves) * LANES, (k % halves + 1) * LANES)
        for f in range(faces):
            direction = precond[k, f].astype(F32) + beta[rows] * dirp[f, rows, lanes]
            new_dir[f, rows, lanes] = direction
            new_lam[f, rows, lanes] = lam[f, rows, lanes] + alpha[rows] * direction
            new_res[f, rows, lanes] = res[f, rows, lanes] - alpha[rows] * image[k, f].astype(F32)
    rho_now[...] = table[0:1, :cases].reshape(cases)
    reduction[...] = table[1:2, :cases].reshape(cases)


def on_device(
    multipliers, residual, dir_prev, rho_prev, face_ids, face_sign,
    dual_blocks, dirichlet_blocks, coupling, corner_ids, coarse_inv,
):
    n_dom, n_blk = lax.axis_size("dom"), lax.axis_size("blk")
    _, faces, cases, face_len = multipliers.shape
    _, subs, local, _ = dual_blocks.shape
    fps = face_ids.shape[2]
    slot_count = subs * fps
    relays = (cases // ROWS) * (face_len // LANES)
    total = n_dom * faces
    ids = jnp.transpose(face_ids, (2, 0, 1))
    signs = jnp.transpose(face_sign, (2, 0, 1))
    code = jnp.arange(n_dom * subs)[None, None, :] * fps + jnp.arange(fps)[:, None, None]
    match = ids[None] == jnp.arange(total)[:, None, None, None]
    first = jnp.min(jnp.where(match, code[None], n_dom * slot_count - 1), axis=(1, 2, 3))
    second = jnp.max(jnp.where(match, code[None], 0), axis=(1, 2, 3))
    span = coarse_inv.shape[2]
    corners = coupling.shape[2]
    share = corners // n_blk
    field = jax.ShapeDtypeStruct((faces, cases, face_len), F32)
    vmem = pl.BlockSpec(memory_space=pltpu.VMEM)
    smem = pl.BlockSpec(memory_space=pltpu.SMEM)
    hbm = pl.BlockSpec(memory_space=pl.ANY)
    dma = pltpu.SemaphoreType.DMA
    terms = pltpu.VMEM((n_blk, subs, cases, share), BF16)
    chunk = (ROWS, LANES)
    owned = jax.ShapeDtypeStruct((relays, faces) + chunk, BF16)
    image, precond, stats = pl.pallas_call(
        step_kernel,
        out_shape=(owned, owned, jax.ShapeDtypeStruct((8, 128), F32)),
        in_specs=[smem] * 4 + [hbm] * 2 + [vmem] * 2 + [hbm] * 4,
        out_specs=(vmem,) * 3,
        scratch_shapes=[
            pltpu.VMEM((subs, local, local), BF16),
            pltpu.VMEM((subs, local, local), BF16),
            pltpu.VMEM((subs, corners, local), BF16),
            pltpu.VMEM((span, span), BF16),
            pltpu.VMEM((faces, cases, face_len), F32),
            pltpu.VMEM((faces, cases, face_len), F32),
            pltpu.VMEM((relays, faces) + chunk, BF16),
            pltpu.VMEM((total,) + chunk, BF16),
            pltpu.VMEM((relays, faces) + chunk, BF16),
            pltpu.VMEM((total,) + chunk, BF16),
            pltpu.VMEM((2, relays, slot_count) + chunk, BF16),
            pltpu.VMEM((2, relays, slot_count) + chunk, BF16),
            pltpu.VMEM((2, relays, slot_count) + chunk, BF16),
            pltpu.VMEM((2, n_dom * slot_count) + chunk, BF16),
            pltpu.VMEM((total,) + chunk, BF16),
            pltpu.VMEM((total,) + chunk, BF16),
            pltpu.VMEM((total,) + chunk, F32),
            pltpu.VMEM((total,) + chunk, F32),
            pltpu.VMEM((total,) + chunk, BF16),
            pltpu.VMEM((2, subs, cases, local), BF16),
            pltpu.VMEM((slot_count, cases, face_len), F32),
            pltpu.VMEM((cases, 128), F32),
            pltpu.VMEM((4, 8, 128), F32),
            pltpu.VMEM((2, n_dom, 8, 128), F32),
            pltpu.VMEM((2, n_blk, 8, 128), F32),
            pltpu.VMEM((128, 128), F32),
            pltpu.VMEM((n_blk, subs, span, share), BF16),
            pltpu.VMEM((2 * n_blk, 8, share), jnp.int32),
            terms, terms, terms, terms,
            dma((6,)),
            dma((8, n_dom - 1)), dma((8, n_dom - 1)),
            dma((4, max(n_dom, n_blk) - 1)), dma((4, max(n_dom, n_blk) - 1)),
            dma((3, n_blk - 1)), dma((3, n_blk - 1)),
        ],
        compiler_params=pltpu.CompilerParams(
            collective_id=0, has_side_effects=True, vmem_limit_bytes=60 << 20
        ),
    )(
        ids, signs, first, second,
        residual[0], dir_prev[0], rho_prev, corner_ids[0],
        dirichlet_blocks[0], dual_blocks[0], coupling[0], coarse_inv[0, 0],
    )
    row = jax.ShapeDtypeStruct((cases,), F32)
    new_lam, new_res, new_dir, rho_now, reduction = pl.pallas_call(
        finish_kernel,
        out_shape=(field, field, field, row, row),
        in_specs=[vmem] * 6,
        out_specs=(vmem,) * 5,
    )(multipliers[0], residual[0], dir_prev[0], precond, image, stats)
    return new_lam[None], new_res[None], new_dir[None], rho_now, reduction


def solution(mesh):
    in_specs = (
        P("blk", "dom", None, None),
        P("blk", "dom", None, None),
        P("blk", "dom", None, None),
        P(),
        P("blk", None, None),
        P("blk", None, None),
        P("blk", "dom", None, None),
        P("blk", "dom", None, None),
        P("blk", "dom", None, None),
        P("blk", "dom", None),
        P("dom", "blk", None, None),
    )
    out_specs = (
        P("blk", "dom", None, None),
        P("blk", "dom", None, None),
        P("blk", "dom", None, None),
        P(),
        P(),
    )
    return jax.shard_map(
        on_device, mesh=mesh, in_specs=in_specs, out_specs=out_specs, check_vma=False
    )
```

```python
import jax
import jax.numpy as jnp
from jax import lax
from jax.experimental import pallas as pl
from jax.experimental.pallas import tpu as pltpu
from jax.sharding import PartitionSpec as P

MESH = pl.DeviceIdType.MESH
F32, BF16 = jnp.float32, jnp.bfloat16
STREAMS = 2
ROWS, LANES = 8, 128
PAIR = (2 * ROWS, LANES)


def remote(src, dst, send, recv, axis, peer):
    return pltpu.make_async_remote_copy(
        src_ref=src, dst_ref=dst, send_sem=send, recv_sem=recv,
        device_id={axis: peer}, device_id_type=MESH,
    )


def pack(one, other):
    return jnp.concatenate([one, other], axis=0).astype(BF16)


def unpack(pair):
    pair = pair.astype(F32)
    return pair[:ROWS], pair[ROWS:]


def lane_sum(value):
    return jnp.sum(value, axis=1, keepdims=True)


def as_column(row, cases):
    tile = jnp.concatenate([row, jnp.zeros((127, row.shape[1]), F32)], axis=0)
    return jnp.transpose(tile)[:cases, :1]


def columns_tile(columns):
    rows = columns[0].shape[0]
    place = lax.broadcasted_iota(jnp.int32, (rows, 128), 1)
    tile = jnp.zeros((rows, 128), F32)
    for i, column in enumerate(columns):
        tile = jnp.where(place == i, column, tile)
    return tile


def step_kernel(
    face_ids, face_sign, first, second,
    res_hbm, dir_hbm, rho_ref, ids_ref,
    dirichlet, dual, coupling, inverse,
    image_in, precond_in, stats,
    w_dir, w_dual, w_cpl, w_inv, res, dirp,
    res_out, res_in, dir_out, dir_in,
    slot_out, slot_in, push_out, push_in, precond_out, image_out,
    held, direction, pushed, slots, products, square,
    part, dom_sums, blk_sums, wide, beta_wide, hot, ids,
    terms_out, terms_in, picks_out, picks_in,
    load, send_x, recv_x, send_s, recv_s, send_t, recv_t,
):
    n_dom, n_blk = lax.axis_size("dom"), lax.axis_size("blk")
    me, my_blk = lax.axis_index("dom"), lax.axis_index("blk")
    faces, cases, face_len = res.shape
    subs = slots.shape[1]
    local = slots.shape[3]
    fps = local // face_len
    slot_count = subs * fps
    half_faces, half_slots = faces // 2, slot_count // 2
    total_faces = n_dom * faces
    stream = cases // STREAMS
    halves = face_len // LANES
    relays = (stream // ROWS) * halves
    group = (me // relays) * relays
    my_chunk = lax.rem(me, relays)
    my_rows = pl.multiple_of((my_chunk // halves) * ROWS, ROWS)
    count = n_dom * n_blk * faces * face_len
    share = w_cpl.shape[1] // n_blk
    span = w_inv.shape[0]
    width = subs * share
    all_peers = [(k - 1, lax.rem(me + k, n_dom)) for k in range(1, n_dom)]
    group_peers = [(k - 1, group + lax.rem(my_chunk + k, relays)) for k in range(1, relays)]
    blk_peers = [(k - 1, lax.rem(my_blk + k, n_blk)) for k in range(1, n_blk)]
    nt = (((1,), (1,)), ((), ()))

    loads = [
        pltpu.make_async_copy(src, dst, load.at[i])
        for i, (src, dst) in enumerate((
            (res_hbm, res), (dirichlet, w_dir), (dir_hbm, dirp),
            (coupling, w_cpl), (dual, w_dual), (inverse, w_inv),
        ))
    ]
    for copy in loads:
        copy.start()

    barrier = pltpu.get_barrier_semaphore()
    for axis, peers in (("dom", all_peers), ("blk", blk_peers)):
        for _, peer in peers:
            pl.semaphore_signal(barrier, inc=1, device_id={axis: peer}, device_id_type=MESH)

    def chunk_of(k):
        q, h = k // halves, k % halves
        return q * ROWS, slice(h * LANES, (h + 1) * LANES)

    def start(copies):
        for copy in copies:
            copy.start()
        return copies

    def finish(copies):
        for copy in copies:
            copy.wait()

    def to_relays(turn, out, into):
        wide_by = out.shape[1]
        copies = start([
            remote(
                out.at[lax.rem(peer, relays)], into.at[pl.ds(me * wide_by, wide_by)],
                send_x.at[turn, k], recv_x.at[turn, k], "dom", peer,
            )
            for k, peer in all_peers
        ])
        into[pl.ds(me * wide_by, wide_by)] = out[my_chunk]
        return copies

    def to_group(turn, source, into):
        copies = start([
            remote(
                source(peer), into.at[my_chunk],
                send_x.at[turn, k], recv_x.at[turn, k], "dom", peer,
            )
            for k, peer in group_peers
        ])
        into[my_chunk] = source(me)[...]
        return copies

    def face_of(d, s):
        return face_ids[s % fps, 0, d * subs + s // fps]

    def sign_of(s):
        return face_sign[s % fps, 0, me * subs + s // fps].astype(F32)

    def split(field, st, put_at):
        for f in range(0, faces, 2):
            for k in range(relays):
                row, lanes = chunk_of(k)
                rows = slice(st * stream + row, st * stream + row + ROWS)
                put_at(k, f // 2, pack(field[f, rows, lanes], field[f + 1, rows, lanes]))

    def hand_out(turn, values):
        for i in range(relays):
            for s in range(0, slot_count, 2):
                slot_out[turn, i, s // 2] = pack(
                    values[face_of(group + i, s)], values[face_of(group + i, s + 1)]
                )
        return to_group(
            turn + 2, lambda peer: slot_out.at[turn, lax.rem(peer, relays)], slot_in.at[turn]
        )

    def to_slots(turn):
        for s in range(0, slot_count, 2):
            for h in range(halves):
                pairs = [
                    unpack(slot_in[turn, q * halves + h, s // 2]) for q in range(relays // halves)
                ]
                for i in range(2):
                    sub, t = divmod(s + i, fps)
                    value = jnp.concatenate([pair[i] for pair in pairs], axis=0) * sign_of(s + i)
                    at = t * face_len + h * LANES
                    slots[turn, sub, :, at:at + LANES] = value.astype(BF16)

    def product(turn, weights, sub, t):
        return jnp.dot(
            slots[turn, sub], weights[sub, :, t * face_len:(t + 1) * face_len],
            preferred_element_type=F32,
        )

    def put(turn, s, one, other):
        for k in range(relays):
            row, lanes = chunk_of(k)
            push_out[turn, k, s // 2] = pack(one[row:row + ROWS, lanes], other[row:row + ROWS, lanes])

    def spread(turn):
        for i in range(n_dom * half_slots):
            pushed[2 * i], pushed[2 * i + 1] = unpack(push_in[turn, i])

    def face_sum(f):
        return pushed[first[f]] + pushed[second[f]]

    def reduce_start(turn, tile, axis, peers, into):
        part[turn] = tile
        here = lax.axis_index(axis)
        copies = start([
            remote(
                part.at[turn], into.at[here], send_s.at[turn, k], recv_s.at[turn, k], axis, peer
            )
            for k, peer in peers
        ])
        into[here] = tile
        return copies

    def reduce_end(copies, into, base, number):
        finish(copies)
        total = into[base]
        for i in range(1, number):
            total = total + into[base + i]
        return total

    loads[0].wait()
    for st in range(STREAMS):
        def put_res(k, i, value, st=st):
            res_out[st, k, i] = value
        split(res, st, put_res)
    pl.semaphore_wait(barrier, n_dom + n_blk - 2)
    pulled = [to_relays(st, res_out.at[st], res_in.at[st]) for st in range(STREAMS)]

    for b in range(n_blk):
        row = [ids_ref[s:s + 1, b * share:(b + 1) * share] for s in range(subs)]
        ids[n_blk + b, 0:1] = jnp.concatenate(row, axis=1) - b * span
    id_copies = start([
        remote(
            ids.at[n_blk + peer], ids.at[my_blk], send_t.at[4, k], recv_t.at[4, k], "blk", peer
        )
        for k, peer in blk_peers
    ])
    ids[my_blk] = ids[n_blk + my_blk]
    total = jnp.zeros((cases, face_len), F32)
    for f in range(faces):
        total += res[f] * res[f]
    square[...] = jnp.broadcast_to(lane_sum(total), (cases, 128))
    loads[2].wait()
    for st in range(STREAMS):
        def put_dir(k, i, value, st=st):
            dir_out[k, st * half_faces + i] = value
        split(dirp, st, put_dir)

    handed = []
    for st in range(STREAMS):
        finish(pulled[st])
        for i in range(n_dom * half_faces):
            held[st, 2 * i], held[st, 2 * i + 1] = unpack(res_in[st, i])
        handed.append(hand_out(st, held.at[st]))
    dir_copies = to_relays(6, dir_out, dir_in)
    finish(id_copies)
    for p in range(n_blk):
        rows = lax.broadcasted_iota(jnp.int32, (span, width), 0)
        hot[:, p * width:(p + 1) * width] = (rows == ids[p, 0:1, :]).astype(F32).astype(BF16)
    loads[1].wait()

    rho_copies, to_sum = [], []
    for st in range(STREAMS):
        finish(handed[st])
        to_slots(st)
        rho_part = jnp.zeros((stream, face_len), F32)
        for s in range(0, slot_count, 2):
            values = []
            for i in range(2):
                sub, t = divmod(s + i, fps)
                value = product(st, w_dir, sub, t)
                values.append(value * sign_of(s + i))
                rho_part += (
                    slots[st, sub, :, t * face_len:(t + 1) * face_len].astype(F32)
                    * value.astype(BF16).astype(F32)
                )
            put(st, s, *values)
        rows = slice(st * stream, (st + 1) * stream)
        tile = columns_tile((lane_sum(rho_part), square[rows, :1]))
        around = [jnp.zeros((st * stream, 128), F32)] if st else []
        after = jnp.zeros((128 - (st + 1) * stream, 128), F32)
        tile = jnp.transpose(jnp.concatenate(around + [tile, after], axis=0))[:8]
        rho_copies.append(reduce_start(st, tile, "dom", all_peers, dom_sums.at[st]))
        to_sum.append(to_relays(7 + st, push_out.at[st], push_in.at[st]))

    pad = jnp.ones((1, 128 - cases), F32)
    rho_prev = jnp.concatenate([rho_ref[...].reshape(1, cases), pad], axis=1)
    rho_now = jnp.zeros((1, 128), F32)
    square_sum = jnp.zeros((1, 128), F32)
    beta_row = jnp.zeros((1, 128), F32)
    for st in range(STREAMS):
        tile = reduce_end(rho_copies[st], dom_sums.at[st], 0, n_dom)
        copies = reduce_start(2 + st, tile, "blk", blk_peers, blk_sums.at[st])
        finish(to_sum[st])
        spread(st)
        if st == 0:
            finish(dir_copies)
        tile = reduce_end(copies, blk_sums.at[st], 0, n_blk)
        rho_now += tile[0:1] / count
        square_sum += tile[1:2]
        row = tile[0:1] / count / rho_prev
        beta_row += row
        column = as_column(row, cases)[st * stream:(st + 1) * stream]
        beta_wide[st] = jnp.broadcast_to(column, (stream, 128))
        beta = beta_wide[st, pl.ds(my_rows, ROWS), :]
        for owner in range(n_dom):
            for i in range(half_faces):
                f = owner * faces + 2 * i
                values = face_sum(f), face_sum(f + 1)
                at = st * half_faces + i
                precond_out[owner, at] = pack(*values)
                before = unpack(dir_in[owner * STREAMS * half_faces + at])
                direction[st, f] = values[0] + beta * before[0]
                direction[st, f + 1] = values[1] + beta * before[1]
        handed[st] = hand_out(2 + st, direction.at[st])
    to_owners = to_group(9, lambda peer: precond_out.at[peer], precond_in)
    for i in (3, 4, 5):
        loads[i].wait()

    def blk_exchange(turn, out, into):
        copies = start([
            remote(out.at[peer], into.at[my_blk], send_t.at[turn, k], recv_t.at[turn, k], "blk", peer)
            for k, peer in blk_peers
        ])
        into[my_blk] = out[my_blk]
        return copies

    def terms(st):
        found = [
            lax.dot_general(slots[2 + st, s], w_cpl[s], nt, preferred_element_type=F32)
            for s in range(subs)
        ]
        for b in range(n_blk):
            terms_out[st, b] = jnp.concatenate(
                [value[:, b * share:(b + 1) * share] for value in found], axis=1
            ).astype(BF16)
        return blk_exchange(st, terms_out.at[st], terms_in.at[st])

    def dual_products(st):
        for s in range(slot_count):
            sub, t = divmod(s, fps)
            products[st, s] = product(2 + st, w_dual, sub, t)

    def solve(st):
        together = jnp.concatenate([terms_in[st, p].astype(F32) for p in range(n_blk)], axis=1)
        rhs = lax.dot_general(together.astype(BF16), hot[...], nt, preferred_element_type=F32)
        solved = jnp.dot(rhs.astype(BF16), w_inv[...], preferred_element_type=F32).astype(BF16)
        picked = jnp.dot(solved, hot[...], preferred_element_type=F32)
        for p in range(n_blk):
            picks_out[st, p] = picked[:, p * width:(p + 1) * width].astype(BF16)
        return blk_exchange(2 + st, picks_out.at[st], picks_in.at[st])

    def rows_out(st):
        for sub in range(subs):
            picked = jnp.concatenate([
                picks_in[st, b].astype(F32)[:, sub * share:(sub + 1) * share] for b in range(n_blk)
            ], axis=1).astype(BF16)
            for t in range(0, fps, 2):
                s = sub * fps + t
                put(2 + st, s, *[
                    (products[st, s + i] + jnp.dot(
                        picked, w_cpl[sub, :, (t + i) * face_len:(t + i + 1) * face_len],
                        preferred_element_type=F32,
                    )) * sign_of(s + i)
                    for i in range(2)
                ])
        return to_relays(10 + st, push_out.at[2 + st], push_in.at[2 + st])

    finish(handed[0])
    to_slots(2)
    first_terms = terms(0)
    dual_products(0)
    finish(first_terms)
    first_picks = solve(0)
    finish(handed[1])
    to_slots(3)
    second_terms = terms(1)
    dual_products(1)
    finish(first_picks)
    to_sum[0] = rows_out(0)
    finish(second_terms)
    second_picks = solve(1)
    finish(second_picks)
    to_sum[1] = rows_out(1)
    wide[...] = jnp.zeros((128, 128), F32)
    finish(to_owners)

    images = []
    for st in range(STREAMS):
        finish(to_sum[st])
        spread(2 + st)
        curve = jnp.zeros((ROWS, LANES), F32)
        cross = jnp.zeros((ROWS, LANES), F32)
        norm = jnp.zeros((ROWS, LANES), F32)
        for owner in range(n_dom):
            for i in range(half_faces):
                f = owner * faces + 2 * i
                values = face_sum(f), face_sum(f + 1)
                image_out[st, owner, i] = pack(*values)
                for j, value in enumerate(values):
                    curve += direction[st, f + j] * value
                    cross += held[st, f + j] * value
                    norm += value * value
        at = pl.multiple_of(st * stream + my_rows, ROWS)
        wide[pl.ds(at, ROWS), :] = columns_tile((lane_sum(curve), lane_sum(cross), lane_sum(norm)))
        if st == STREAMS - 1:
            tile = jnp.transpose(wide[...])[:8]
            copies = reduce_start(4, tile, "dom", group_peers, dom_sums.at[2])
        images.append(to_group(
            12 + st, lambda peer: image_out.at[st, peer], image_in.at[st]
        ))
    tile = reduce_end(copies, dom_sums.at[2], group, relays)
    copies = reduce_start(5, tile, "blk", blk_peers, blk_sums.at[2])
    tile = reduce_end(copies, blk_sums.at[2], 0, n_blk)
    alpha = rho_now / (tile[0:1] / count)
    new_sum = square_sum - 2.0 * alpha * tile[1:2] + alpha * alpha * tile[2:3]
    stats[0:1] = rho_now
    stats[1:2] = (new_sum / count) / (square_sum / count)
    stats[2:3] = alpha
    stats[3:4] = beta_row
    stats[4:8] = jnp.zeros((4, 128), F32)
    for copies in images:
        finish(copies)


def finish_kernel(
    lam, res, dirp, precond, image, stats, new_lam, new_res, new_dir, rho_now, reduction
):
    faces, cases, face_len = lam.shape
    halves = face_len // LANES
    stream = cases // STREAMS
    table = stats[...]
    alpha = as_column(table[2:3], cases)
    beta = as_column(table[3:4], cases)
    for st in range(STREAMS):
        for k in range(precond.shape[0]):
            row = st * stream + (k // halves) * ROWS
            rows = slice(row, row + ROWS)
            lanes = slice((k % halves) * LANES, (k % halves + 1) * LANES)
            for i in range(faces // 2):
                sums = unpack(precond[k, st * (faces // 2) + i])
                images = unpack(image[st, k, i])
                for j in range(2):
                    f = 2 * i + j
                    direction = sums[j] + beta[rows] * dirp[f, rows, lanes]
                    new_dir[f, rows, lanes] = direction
                    new_lam[f, rows, lanes] = lam[f, rows, lanes] + alpha[rows] * direction
                    new_res[f, rows, lanes] = res[f, rows, lanes] - alpha[rows] * images[j]
    rho_now[...] = table[0:1, :cases].reshape(cases)
    reduction[...] = table[1:2, :cases].reshape(cases)


def on_device(
    multipliers, residual, dir_prev, rho_prev, face_ids, face_sign,
    dual_blocks, dirichlet_blocks, coupling, corner_ids, coarse_inv,
):
    n_dom, n_blk = lax.axis_size("dom"), lax.axis_size("blk")
    _, faces, cases, face_len = multipliers.shape
    _, subs, local, _ = dual_blocks.shape
    fps = face_ids.shape[2]
    slot_count = subs * fps
    stream = cases // STREAMS
    relays = (stream // ROWS) * (face_len // LANES)
    total = n_dom * faces
    ids = jnp.transpose(face_ids, (2, 0, 1))
    signs = jnp.transpose(face_sign, (2, 0, 1))
    code = jnp.arange(n_dom * subs)[None, None, :] * fps + jnp.arange(fps)[:, None, None]
    match = ids[None] == jnp.arange(total)[:, None, None, None]
    first = jnp.min(jnp.where(match, code[None], n_dom * slot_count - 1), axis=(1, 2, 3))
    second = jnp.max(jnp.where(match, code[None], 0), axis=(1, 2, 3))
    span = coarse_inv.shape[2]
    corners = coupling.shape[2]
    width = subs * (corners // n_blk)
    half_faces, half_slots = faces // 2, slot_count // 2
    field = jax.ShapeDtypeStruct((faces, cases, face_len), F32)
    vmem = pl.BlockSpec(memory_space=pltpu.VMEM)
    smem = pl.BlockSpec(memory_space=pltpu.SMEM)
    hbm = pl.BlockSpec(memory_space=pl.ANY)
    dma = pltpu.SemaphoreType.DMA
    terms = pltpu.VMEM((STREAMS, n_blk, stream, width), BF16)
    chunk = (ROWS, LANES)
    image, precond, stats = pl.pallas_call(
        step_kernel,
        out_shape=(
            jax.ShapeDtypeStruct((STREAMS, relays, half_faces) + PAIR, BF16),
            jax.ShapeDtypeStruct((relays, STREAMS * half_faces) + PAIR, BF16),
            jax.ShapeDtypeStruct((8, 128), F32),
        ),
        in_specs=[smem] * 4 + [hbm] * 2 + [vmem] * 2 + [hbm] * 4,
        out_specs=(vmem,) * 3,
        scratch_shapes=[
            pltpu.VMEM((subs, local, local), BF16),
            pltpu.VMEM((subs, local, local), BF16),
            pltpu.VMEM((subs, corners, local), BF16),
            pltpu.VMEM((span, span), BF16),
            pltpu.VMEM((faces, cases, face_len), F32),
            pltpu.VMEM((faces, cases, face_len), F32),
            pltpu.VMEM((STREAMS, relays, half_faces) + PAIR, BF16),
            pltpu.VMEM((STREAMS, n_dom * half_faces) + PAIR, BF16),
            pltpu.VMEM((relays, STREAMS * half_faces) + PAIR, BF16),
            pltpu.VMEM((n_dom * STREAMS * half_faces,) + PAIR, BF16),
            pltpu.VMEM((2 * STREAMS, relays, half_slots) + PAIR, BF16),
            pltpu.VMEM((2 * STREAMS, relays, half_slots) + PAIR, BF16),
            pltpu.VMEM((2 * STREAMS, relays, half_slots) + PAIR, BF16),
            pltpu.VMEM((2 * STREAMS, n_dom * half_slots) + PAIR, BF16),
            pltpu.VMEM((n_dom, STREAMS * half_faces) + PAIR, BF16),
            pltpu.VMEM((STREAMS, n_dom, half_faces) + PAIR, BF16),
            pltpu.VMEM((STREAMS, total) + chunk, F32),
            pltpu.VMEM((STREAMS, total) + chunk, F32),
            pltpu.VMEM((n_dom * slot_count,) + chunk, F32),
            pltpu.VMEM((2 * STREAMS, subs, stream, local), BF16),
            pltpu.VMEM((STREAMS, slot_count, stream, face_len), F32),
            pltpu.VMEM((cases, 128), F32),
            pltpu.VMEM((6, 8, 128), F32),
            pltpu.VMEM((3, n_dom, 8, 128), F32),
            pltpu.VMEM((3, n_blk, 8, 128), F32),
            pltpu.VMEM((128, 128), F32),
            pltpu.VMEM((STREAMS, stream, 128), F32),
            pltpu.VMEM((span, n_blk * width), BF16),
            pltpu.VMEM((2 * n_blk, 8, width), jnp.int32),
            terms, terms, terms, terms,
            dma((6,)),
            dma((14, n_dom - 1)), dma((14, n_dom - 1)),
            dma((6, max(n_dom, n_blk) - 1)), dma((6, max(n_dom, n_blk) - 1)),
            dma((5, n_blk - 1)), dma((5, n_blk - 1)),
        ],
        compiler_params=pltpu.CompilerParams(
            collective_id=0, has_side_effects=True, vmem_limit_bytes=60 << 20
        ),
    )(
        ids, signs, first, second,
        residual[0], dir_prev[0], rho_prev, corner_ids[0],
        dirichlet_blocks[0], dual_blocks[0], coupling[0], coarse_inv[0, 0],
    )
    row = jax.ShapeDtypeStruct((cases,), F32)
    new_lam, new_res, new_dir, rho_now, reduction = pl.pallas_call(
        finish_kernel,
        out_shape=(field, field, field, row, row),
        in_specs=[vmem] * 6,
        out_specs=(vmem,) * 5,
    )(multipliers[0], residual[0], dir_prev[0], precond, image, stats)
    return new_lam[None], new_res[None], new_dir[None], rho_now, reduction


def solution(mesh):
    in_specs = (
        P("blk", "dom", None, None),
        P("blk", "dom", None, None),
        P("blk", "dom", None, None),
        P(),
        P("blk", None, None),
        P("blk", None, None),
        P("blk", "dom", None, None),
        P("blk", "dom", None, None),
        P("blk", "dom", None, None),
        P("blk", "dom", None),
        P("dom", "blk", None, None),
    )
    out_specs = (
        P("blk", "dom", None, None),
        P("blk", "dom", None, None),
        P("blk", "dom", None, None),
        P(),
        P(),
    )
    return jax.shard_map(
        on_device, mesh=mesh, in_specs=in_specs, out_specs=out_specs, check_vma=False
    )
```

```python
import jax
import jax.numpy as jnp
from jax import lax
from jax.experimental import pallas as pl
from jax.experimental.pallas import tpu as pltpu
from jax.sharding import PartitionSpec as P

MESH = pl.DeviceIdType.MESH
F32, BF16 = jnp.float32, jnp.bfloat16
STREAMS = 2
ROWS, LANES = 8, 128
PAIR = (2 * ROWS, LANES)


def remote(src, dst, send, recv, axis, peer):
    return pltpu.make_async_remote_copy(
        src_ref=src, dst_ref=dst, send_sem=send, recv_sem=recv,
        device_id={axis: peer}, device_id_type=MESH,
    )


def pack(one, other):
    return jnp.concatenate([one, other], axis=0).astype(BF16)


def unpack(pair):
    pair = pair.astype(F32)
    return pair[:ROWS], pair[ROWS:]


def lane_sum(value):
    return jnp.sum(value, axis=1, keepdims=True)


def as_column(row, cases):
    tile = jnp.concatenate([row, jnp.zeros((127, row.shape[1]), F32)], axis=0)
    return jnp.transpose(tile)[:cases, :1]


def columns_tile(columns):
    rows = columns[0].shape[0]
    place = lax.broadcasted_iota(jnp.int32, (rows, 128), 1)
    tile = jnp.zeros((rows, 128), F32)
    for i, column in enumerate(columns):
        tile = jnp.where(place == i, column, tile)
    return tile


def step_kernel(
    face_ids, face_sign, first, second,
    res_hbm, dir_hbm, rho_ref, ids_ref,
    dirichlet, dual, coupling, inverse,
    image_in, precond_in, stats,
    w_dir, w_dual, w_cpl, w_inv, res, dirp,
    res_out, res_in, dir_out, dir_in,
    pull_out, pull_in, slot_out, slot_in, push_out, push_in, precond_out, image_out,
    held, direction, pushed, slots, products, square,
    part, dom_sums, blk_sums, wide, beta_wide, hot, ids,
    terms_out, terms_in, picks_out, picks_in,
    load, send_x, recv_x, send_s, recv_s, send_t, recv_t,
):
    n_dom, n_blk = lax.axis_size("dom"), lax.axis_size("blk")
    me, my_blk = lax.axis_index("dom"), lax.axis_index("blk")
    faces, cases, face_len = res.shape
    subs = slots.shape[1]
    local = slots.shape[3]
    fps = local // face_len
    slot_count = subs * fps
    half_faces, half_slots = faces // 2, slot_count // 2
    total_faces = n_dom * faces
    stream = cases // STREAMS
    halves = face_len // LANES
    quarters = stream // ROWS
    relays = quarters * halves
    group = (me // relays) * relays
    my_chunk = lax.rem(me, relays)
    quarter = lax.rem(me, quarters)
    my_rows = pl.multiple_of(quarter * ROWS, ROWS)
    my_lanes = pl.multiple_of((my_chunk // quarters) * LANES, LANES)
    count = n_dom * n_blk * faces * face_len
    share = w_cpl.shape[1] // n_blk
    span = w_inv.shape[0]
    width = subs * share
    all_peers = [(k - 1, lax.rem(me + k, n_dom)) for k in range(1, n_dom)]
    group_peers = [(k - 1, group + lax.rem(my_chunk + k, relays)) for k in range(1, relays)]
    near = (me // quarters) * quarters
    near_peers = [(k - 1, near + lax.rem(quarter + k, quarters)) for k in range(1, quarters)]
    blk_peers = [(k - 1, lax.rem(my_blk + k, n_blk)) for k in range(1, n_blk)]
    nt = (((1,), (1,)), ((), ()))

    loads = [
        pltpu.make_async_copy(src, dst, load.at[i])
        for i, (src, dst) in enumerate((
            (res_hbm, res), (dirichlet, w_dir), (dir_hbm, dirp),
            (coupling, w_cpl), (dual, w_dual), (inverse, w_inv),
        ))
    ]
    for copy in loads:
        copy.start()

    barrier = pltpu.get_barrier_semaphore()
    for axis, peers in (("dom", all_peers), ("blk", blk_peers)):
        for _, peer in peers:
            pl.semaphore_signal(barrier, inc=1, device_id={axis: peer}, device_id_type=MESH)

    def chunk_of(k):
        h, q = k // quarters, k % quarters
        return q * ROWS, slice(h * LANES, (h + 1) * LANES)

    def start(copies):
        for copy in copies:
            copy.start()
        return copies

    def finish(copies):
        for copy in copies:
            copy.wait()

    def to_relays(turn, out, into):
        chunks, wide_by = out.shape[:2]
        copies = start([
            remote(
                out.at[lax.rem(peer, chunks)], into.at[pl.ds(me * wide_by, wide_by)],
                send_x.at[turn, k], recv_x.at[turn, k], "dom", peer,
            )
            for k, peer in all_peers
        ])
        into[pl.ds(me * wide_by, wide_by)] = out[lax.rem(me, chunks)]
        return copies

    def to_group(turn, source, into, peers=group_peers, here=my_chunk):
        copies = start([
            remote(
                source(peer), into.at[here],
                send_x.at[turn, k], recv_x.at[turn, k], "dom", peer,
            )
            for k, peer in peers
        ])
        into[here] = source(me)[...]
        return copies

    def face_of(d, s):
        return face_ids[s % fps, 0, d * subs + s // fps]

    def sign_of(s):
        return face_sign[s % fps, 0, me * subs + s // fps].astype(F32)

    def hand_out(turn, values):
        for i in range(relays):
            for s in range(0, slot_count, 2):
                slot_out[turn, i, s // 2] = pack(
                    values[face_of(group + i, s)], values[face_of(group + i, s + 1)]
                )
        return to_group(
            turn + 4, lambda peer: slot_out.at[turn, lax.rem(peer, relays)], slot_in.at[turn]
        )

    def to_slots(turn):
        for s in range(0, slot_count, 2):
            for h in range(halves):
                pairs = [
                    unpack(slot_in[turn, h * quarters + q, s // 2]) for q in range(quarters)
                ]
                for i in range(2):
                    sub, t = divmod(s + i, fps)
                    value = jnp.concatenate([pair[i] for pair in pairs], axis=0) * sign_of(s + i)
                    at = t * face_len + h * LANES
                    slots[STREAMS + turn, sub, :, at:at + LANES] = value.astype(BF16)

    def pulled_slots(st):
        for s in range(0, slot_count, 2):
            pairs = [unpack(pull_in[st, q, s // 2]) for q in range(quarters)]
            for i in range(2):
                sub, t = divmod(s + i, fps)
                value = jnp.concatenate([pair[i] for pair in pairs], axis=0) * sign_of(s + i)
                slots[st, sub, :, t * face_len:(t + 1) * face_len] = value.astype(BF16)

    def product(turn, weights, sub, t):
        return jnp.dot(
            slots[turn, sub], weights[sub, :, t * face_len:(t + 1) * face_len],
            preferred_element_type=F32,
        )

    def put(turn, s, one, other):
        for k in range(relays):
            row, lanes = chunk_of(k)
            push_out[turn, k, s // 2] = pack(one[row:row + ROWS, lanes], other[row:row + ROWS, lanes])

    def spread(turn):
        for i in range(n_dom * half_slots):
            pushed[2 * i], pushed[2 * i + 1] = unpack(push_in[turn, i])

    def face_sum(f):
        return pushed[first[f]] + pushed[second[f]]

    def reduce_start(turn, tile, axis, peers, into):
        part[turn] = tile
        here = lax.axis_index(axis)
        copies = start([
            remote(
                part.at[turn], into.at[here], send_s.at[turn, k], recv_s.at[turn, k], axis, peer
            )
            for k, peer in peers
        ])
        into[here] = tile
        return copies

    def reduce_end(copies, into, base, number):
        finish(copies)
        total = into[base]
        for i in range(1, number):
            total = total + into[base + i]
        return total

    loads[0].wait()
    for st in range(STREAMS):
        for f in range(0, faces, 2):
            for q in range(quarters):
                rows = slice(st * stream + q * ROWS, st * stream + (q + 1) * ROWS)
                res_out[st, q, f // 2] = pack(res[f, rows], res[f + 1, rows])
    pl.semaphore_wait(barrier, n_dom + n_blk - 2)
    pulled = [to_relays(st, res_out.at[st], res_in.at[st]) for st in range(STREAMS)]

    for b in range(n_blk):
        row = [ids_ref[s:s + 1, b * share:(b + 1) * share] for s in range(subs)]
        ids[n_blk + b, 0:1] = jnp.concatenate(row, axis=1) - b * span
    id_copies = start([
        remote(
            ids.at[n_blk + peer], ids.at[my_blk], send_t.at[4, k], recv_t.at[4, k], "blk", peer
        )
        for k, peer in blk_peers
    ])
    ids[my_blk] = ids[n_blk + my_blk]
    total = jnp.zeros((cases, face_len), F32)
    for f in range(faces):
        total += res[f] * res[f]
    square[...] = jnp.broadcast_to(lane_sum(total), (cases, 128))
    loads[2].wait()
    for st in range(STREAMS):
        for f in range(0, faces, 2):
            for k in range(relays):
                row, lanes = chunk_of(k)
                rows = slice(st * stream + row, st * stream + row + ROWS)
                dir_out[k, st * half_faces + f // 2] = pack(
                    dirp[f, rows, lanes], dirp[f + 1, rows, lanes]
                )

    handed = []
    for st in range(STREAMS):
        finish(pulled[st])
        for i in range(n_dom * half_faces):
            held[st, 2 * i], held[st, 2 * i + 1] = unpack(res_in[st, i])
        for i in range(quarters):
            for s in range(0, slot_count, 2):
                pull_out[st, i, s // 2] = pack(
                    held[st, face_of(near + i, s)], held[st, face_of(near + i, s + 1)]
                )
        handed.append(to_group(
            2 + st, lambda peer: pull_out.at[st, lax.rem(peer, quarters)], pull_in.at[st],
            near_peers, quarter,
        ))
    dir_copies = to_relays(6, dir_out, dir_in)
    finish(id_copies)
    for p in range(n_blk):
        rows = lax.broadcasted_iota(jnp.int32, (span, width), 0)
        hot[:, p * width:(p + 1) * width] = (rows == ids[p, 0:1, :]).astype(F32).astype(BF16)
    loads[1].wait()

    rho_copies, to_sum = [], []
    for st in range(STREAMS):
        finish(handed[st])
        pulled_slots(st)
        rho_part = jnp.zeros((stream, face_len), F32)
        for s in range(0, slot_count, 2):
            values = []
            for i in range(2):
                sub, t = divmod(s + i, fps)
                value = product(st, w_dir, sub, t)
                values.append(value * sign_of(s + i))
                rho_part += (
                    slots[st, sub, :, t * face_len:(t + 1) * face_len].astype(F32)
                    * value.astype(BF16).astype(F32)
                )
            put(st, s, *values)
        rows = slice(st * stream, (st + 1) * stream)
        tile = columns_tile((lane_sum(rho_part), square[rows, :1]))
        around = [jnp.zeros((st * stream, 128), F32)] if st else []
        after = jnp.zeros((128 - (st + 1) * stream, 128), F32)
        tile = jnp.transpose(jnp.concatenate(around + [tile, after], axis=0))[:8]
        rho_copies.append(reduce_start(st, tile, "dom", all_peers, dom_sums.at[st]))
        to_sum.append(to_relays(7 + st, push_out.at[st], push_in.at[st]))

    pad = jnp.ones((1, 128 - cases), F32)
    rho_prev = jnp.concatenate([rho_ref[...].reshape(1, cases), pad], axis=1)
    rho_now = jnp.zeros((1, 128), F32)
    square_sum = jnp.zeros((1, 128), F32)
    beta_row = jnp.zeros((1, 128), F32)
    for st in range(STREAMS):
        tile = reduce_end(rho_copies[st], dom_sums.at[st], 0, n_dom)
        copies = reduce_start(2 + st, tile, "blk", blk_peers, blk_sums.at[st])
        finish(to_sum[st])
        spread(st)
        if st == 0:
            finish(dir_copies)
        tile = reduce_end(copies, blk_sums.at[st], 0, n_blk)
        rho_now += tile[0:1] / count
        square_sum += tile[1:2]
        row = tile[0:1] / count / rho_prev
        beta_row += row
        column = as_column(row, cases)[st * stream:(st + 1) * stream]
        beta_wide[st] = jnp.broadcast_to(column, (stream, 128))
        beta = beta_wide[st, pl.ds(my_rows, ROWS), :]
        for owner in range(n_dom):
            for i in range(half_faces):
                f = owner * faces + 2 * i
                values = face_sum(f), face_sum(f + 1)
                at = st * half_faces + i
                precond_out[owner, at] = pack(*values)
                before = unpack(dir_in[owner * STREAMS * half_faces + at])
                direction[st, f] = values[0] + beta * before[0]
                direction[st, f + 1] = values[1] + beta * before[1]
        handed[st] = hand_out(st, direction.at[st])
    to_owners = to_group(9, lambda peer: precond_out.at[peer], precond_in)
    for i in (3, 4, 5):
        loads[i].wait()

    def blk_exchange(turn, out, into):
        copies = start([
            remote(out.at[peer], into.at[my_blk], send_t.at[turn, k], recv_t.at[turn, k], "blk", peer)
            for k, peer in blk_peers
        ])
        into[my_blk] = out[my_blk]
        return copies

    def terms(st):
        found = [
            lax.dot_general(slots[2 + st, s], w_cpl[s], nt, preferred_element_type=F32)
            for s in range(subs)
        ]
        for b in range(n_blk):
            terms_out[st, b] = jnp.concatenate(
                [value[:, b * share:(b + 1) * share] for value in found], axis=1
            ).astype(BF16)
        return blk_exchange(st, terms_out.at[st], terms_in.at[st])

    def dual_products(st):
        for s in range(slot_count):
            sub, t = divmod(s, fps)
            products[st, s] = product(2 + st, w_dual, sub, t)

    def solve(st):
        together = jnp.concatenate([terms_in[st, p].astype(F32) for p in range(n_blk)], axis=1)
        rhs = lax.dot_general(together.astype(BF16), hot[...], nt, preferred_element_type=F32)
        solved = jnp.dot(rhs.astype(BF16), w_inv[...], preferred_element_type=F32).astype(BF16)
        picked = jnp.dot(solved, hot[...], preferred_element_type=F32)
        for p in range(n_blk):
            picks_out[st, p] = picked[:, p * width:(p + 1) * width].astype(BF16)
        return blk_exchange(2 + st, picks_out.at[st], picks_in.at[st])

    def rows_out(st):
        for sub in range(subs):
            picked = jnp.concatenate([
                picks_in[st, b].astype(F32)[:, sub * share:(sub + 1) * share] for b in range(n_blk)
            ], axis=1).astype(BF16)
            for t in range(0, fps, 2):
                s = sub * fps + t
                put(2 + st, s, *[
                    (products[st, s + i] + jnp.dot(
                        picked, w_cpl[sub, :, (t + i) * face_len:(t + i + 1) * face_len],
                        preferred_element_type=F32,
                    )) * sign_of(s + i)
                    for i in range(2)
                ])
        return to_relays(10 + st, push_out.at[2 + st], push_in.at[2 + st])

    finish(handed[0])
    to_slots(0)
    first_terms = terms(0)
    dual_products(0)
    finish(first_terms)
    first_picks = solve(0)
    finish(handed[1])
    to_slots(1)
    second_terms = terms(1)
    dual_products(1)
    finish(first_picks)
    to_sum[0] = rows_out(0)
    finish(second_terms)
    second_picks = solve(1)
    finish(second_picks)
    to_sum[1] = rows_out(1)
    wide[...] = jnp.zeros((128, 128), F32)
    finish(to_owners)

    images = []
    for st in range(STREAMS):
        finish(to_sum[st])
        spread(2 + st)
        curve = jnp.zeros((ROWS, LANES), F32)
        cross = jnp.zeros((ROWS, LANES), F32)
        norm = jnp.zeros((ROWS, LANES), F32)
        for owner in range(n_dom):
            for i in range(half_faces):
                f = owner * faces + 2 * i
                values = face_sum(f), face_sum(f + 1)
                image_out[st, owner, i] = pack(*values)
                for j, value in enumerate(values):
                    curve += direction[st, f + j] * value
                    cross += held[st, f + j, :, pl.ds(my_lanes, LANES)] * value
                    norm += value * value
        at = pl.multiple_of(st * stream + my_rows, ROWS)
        wide[pl.ds(at, ROWS), :] = columns_tile((lane_sum(curve), lane_sum(cross), lane_sum(norm)))
        if st == STREAMS - 1:
            tile = jnp.transpose(wide[...])[:8]
            copies = reduce_start(4, tile, "dom", group_peers, dom_sums.at[2])
        images.append(to_group(
            12 + st, lambda peer: image_out.at[st, peer], image_in.at[st]
        ))
    tile = reduce_end(copies, dom_sums.at[2], group, relays)
    copies = reduce_start(5, tile, "blk", blk_peers, blk_sums.at[2])
    tile = reduce_end(copies, blk_sums.at[2], 0, n_blk)
    alpha = rho_now / (tile[0:1] / count)
    new_sum = square_sum - 2.0 * alpha * tile[1:2] + alpha * alpha * tile[2:3]
    stats[0:1] = rho_now
    stats[1:2] = (new_sum / count) / (square_sum / count)
    stats[2:3] = alpha
    stats[3:4] = beta_row
    stats[4:8] = jnp.zeros((4, 128), F32)
    for copies in images:
        finish(copies)


def finish_kernel(
    lam, res, dirp, precond, image, stats, new_lam, new_res, new_dir, rho_now, reduction
):
    faces, cases, face_len = lam.shape
    stream = cases // STREAMS
    quarters = stream // ROWS
    table = stats[...]
    alpha = as_column(table[2:3], cases)
    beta = as_column(table[3:4], cases)
    for st in range(STREAMS):
        for k in range(precond.shape[0]):
            row = st * stream + (k % quarters) * ROWS
            rows = slice(row, row + ROWS)
            lanes = slice((k // quarters) * LANES, (k // quarters + 1) * LANES)
            for i in range(faces // 2):
                sums = unpack(precond[k, st * (faces // 2) + i])
                images = unpack(image[st, k, i])
                for j in range(2):
                    f = 2 * i + j
                    direction = sums[j] + beta[rows] * dirp[f, rows, lanes]
                    new_dir[f, rows, lanes] = direction
                    new_lam[f, rows, lanes] = lam[f, rows, lanes] + alpha[rows] * direction
                    new_res[f, rows, lanes] = res[f, rows, lanes] - alpha[rows] * images[j]
    rho_now[...] = table[0:1, :cases].reshape(cases)
    reduction[...] = table[1:2, :cases].reshape(cases)


def on_device(
    multipliers, residual, dir_prev, rho_prev, face_ids, face_sign,
    dual_blocks, dirichlet_blocks, coupling, corner_ids, coarse_inv,
):
    n_dom, n_blk = lax.axis_size("dom"), lax.axis_size("blk")
    _, faces, cases, face_len = multipliers.shape
    _, subs, local, _ = dual_blocks.shape
    fps = face_ids.shape[2]
    slot_count = subs * fps
    stream = cases // STREAMS
    quarters = stream // ROWS
    relays = quarters * (face_len // LANES)
    total = n_dom * faces
    ids = jnp.transpose(face_ids, (2, 0, 1))
    signs = jnp.transpose(face_sign, (2, 0, 1))
    code = jnp.arange(n_dom * subs)[None, None, :] * fps + jnp.arange(fps)[:, None, None]
    match = ids[None] == jnp.arange(total)[:, None, None, None]
    first = jnp.min(jnp.where(match, code[None], n_dom * slot_count - 1), axis=(1, 2, 3))
    second = jnp.max(jnp.where(match, code[None], 0), axis=(1, 2, 3))
    span = coarse_inv.shape[2]
    corners = coupling.shape[2]
    width = subs * (corners // n_blk)
    half_faces, half_slots = faces // 2, slot_count // 2
    field = jax.ShapeDtypeStruct((faces, cases, face_len), F32)
    vmem = pl.BlockSpec(memory_space=pltpu.VMEM)
    smem = pl.BlockSpec(memory_space=pltpu.SMEM)
    hbm = pl.BlockSpec(memory_space=pl.ANY)
    dma = pltpu.SemaphoreType.DMA
    terms = pltpu.VMEM((STREAMS, n_blk, stream, width), BF16)
    chunk = (ROWS, LANES)
    image, precond, stats = pl.pallas_call(
        step_kernel,
        out_shape=(
            jax.ShapeDtypeStruct((STREAMS, relays, half_faces) + PAIR, BF16),
            jax.ShapeDtypeStruct((relays, STREAMS * half_faces) + PAIR, BF16),
            jax.ShapeDtypeStruct((8, 128), F32),
        ),
        in_specs=[smem] * 4 + [hbm] * 2 + [vmem] * 2 + [hbm] * 4,
        out_specs=(vmem,) * 3,
        scratch_shapes=[
            pltpu.VMEM((subs, local, local), BF16),
            pltpu.VMEM((subs, local, local), BF16),
            pltpu.VMEM((subs, corners, local), BF16),
            pltpu.VMEM((span, span), BF16),
            pltpu.VMEM((faces, cases, face_len), F32),
            pltpu.VMEM((faces, cases, face_len), F32),
            pltpu.VMEM((STREAMS, quarters, half_faces, 2 * ROWS, face_len), BF16),
            pltpu.VMEM((STREAMS, n_dom * half_faces, 2 * ROWS, face_len), BF16),
            pltpu.VMEM((relays, STREAMS * half_faces) + PAIR, BF16),
            pltpu.VMEM((n_dom * STREAMS * half_faces,) + PAIR, BF16),
            pltpu.VMEM((STREAMS, quarters, half_slots, 2 * ROWS, face_len), BF16),
            pltpu.VMEM((STREAMS, quarters, half_slots, 2 * ROWS, face_len), BF16),
            pltpu.VMEM((STREAMS, relays, half_slots) + PAIR, BF16),
            pltpu.VMEM((STREAMS, relays, half_slots) + PAIR, BF16),
            pltpu.VMEM((2 * STREAMS, relays, half_slots) + PAIR, BF16),
            pltpu.VMEM((2 * STREAMS, n_dom * half_slots) + PAIR, BF16),
            pltpu.VMEM((n_dom, STREAMS * half_faces) + PAIR, BF16),
            pltpu.VMEM((STREAMS, n_dom, half_faces) + PAIR, BF16),
            pltpu.VMEM((STREAMS, total, ROWS, face_len), F32),
            pltpu.VMEM((STREAMS, total) + chunk, F32),
            pltpu.VMEM((n_dom * slot_count,) + chunk, F32),
            pltpu.VMEM((2 * STREAMS, subs, stream, local), BF16),
            pltpu.VMEM((STREAMS, slot_count, stream, face_len), F32),
            pltpu.VMEM((cases, 128), F32),
            pltpu.VMEM((6, 8, 128), F32),
            pltpu.VMEM((3, n_dom, 8, 128), F32),
            pltpu.VMEM((3, n_blk, 8, 128), F32),
            pltpu.VMEM((128, 128), F32),
            pltpu.VMEM((STREAMS, stream, 128), F32),
            pltpu.VMEM((span, n_blk * width), BF16),
            pltpu.VMEM((2 * n_blk, 8, width), jnp.int32),
            terms, terms, terms, terms,
            dma((6,)),
            dma((14, n_dom - 1)), dma((14, n_dom - 1)),
            dma((6, max(n_dom, n_blk) - 1)), dma((6, max(n_dom, n_blk) - 1)),
            dma((5, n_blk - 1)), dma((5, n_blk - 1)),
        ],
        compiler_params=pltpu.CompilerParams(
            collective_id=0, has_side_effects=True, vmem_limit_bytes=60 << 20
        ),
    )(
        ids, signs, first, second,
        residual[0], dir_prev[0], rho_prev, corner_ids[0],
        dirichlet_blocks[0], dual_blocks[0], coupling[0], coarse_inv[0, 0],
    )
    row = jax.ShapeDtypeStruct((cases,), F32)
    new_lam, new_res, new_dir, rho_now, reduction = pl.pallas_call(
        finish_kernel,
        out_shape=(field, field, field, row, row),
        in_specs=[vmem] * 6,
        out_specs=(vmem,) * 5,
    )(multipliers[0], residual[0], dir_prev[0], precond, image, stats)
    return new_lam[None], new_res[None], new_dir[None], rho_now, reduction


def solution(mesh):
    in_specs = (
        P("blk", "dom", None, None),
        P("blk", "dom", None, None),
        P("blk", "dom", None, None),
        P(),
        P("blk", None, None),
        P("blk", None, None),
        P("blk", "dom", None, None),
        P("blk", "dom", None, None),
        P("blk", "dom", None, None),
        P("blk", "dom", None),
        P("dom", "blk", None, None),
    )
    out_specs = (
        P("blk", "dom", None, None),
        P("blk", "dom", None, None),
        P("blk", "dom", None, None),
        P(),
        P(),
    )
    return jax.shard_map(
        on_device, mesh=mesh, in_specs=in_specs, out_specs=out_specs, check_vma=False
    )
```

```python
import jax
import jax.numpy as jnp
from jax import lax
from jax.experimental import pallas as pl
from jax.experimental.pallas import tpu as pltpu
from jax.sharding import PartitionSpec as P

MESH = pl.DeviceIdType.MESH
F32, BF16 = jnp.float32, jnp.bfloat16
STREAMS = 2
ROWS, LANES = 8, 128
PAIR = (2 * ROWS, LANES)


def remote(src, dst, send, recv, axis, peer):
    return pltpu.make_async_remote_copy(
        src_ref=src, dst_ref=dst, send_sem=send, recv_sem=recv,
        device_id={axis: peer}, device_id_type=MESH,
    )


def pack(one, other):
    return jnp.concatenate([one, other], axis=0).astype(BF16)


def unpack(pair):
    pair = pair.astype(F32)
    return pair[:ROWS], pair[ROWS:]


def lane_sum(value):
    return jnp.sum(value, axis=1, keepdims=True)


def as_column(row, cases):
    tile = jnp.concatenate([row, jnp.zeros((127, row.shape[1]), F32)], axis=0)
    return jnp.transpose(tile)[:cases, :1]


def columns_tile(columns):
    rows = columns[0].shape[0]
    place = lax.broadcasted_iota(jnp.int32, (rows, 128), 1)
    tile = jnp.zeros((rows, 128), F32)
    for i, column in enumerate(columns):
        tile = jnp.where(place == i, column, tile)
    return tile


def step_kernel(
    face_ids, face_sign,
    id_rows, res_hbm, dir_hbm, rho_ref, ids_ref,
    dirichlet, dual, coupling, inverse,
    image_in, precond_in, stats,
    w_dir, w_dual, w_cpl, w_inv, res, dirp,
    res_out, res_in, dir_out, dir_in,
    pull_out, pull_in, slot_out, slot_in, push_out, push_in, precond_out, image_out,
    held, direction, pushed, slots, products, square,
    part, dom_sums, blk_sums, wide, beta_wide, hot, ids,
    terms_out, terms_in, picks_out, picks_in,
    table, first, second, load, send_x, recv_x, send_s, recv_s, send_t, recv_t,
):
    n_dom, n_blk = lax.axis_size("dom"), lax.axis_size("blk")
    me, my_blk = lax.axis_index("dom"), lax.axis_index("blk")
    faces, cases, face_len = res.shape
    subs = slots.shape[1]
    local = slots.shape[3]
    fps = local // face_len
    slot_count = subs * fps
    half_faces, half_slots = faces // 2, slot_count // 2
    total_faces = n_dom * faces
    stream = cases // STREAMS
    halves = face_len // LANES
    quarters = stream // ROWS
    relays = quarters * halves
    group = (me // relays) * relays
    my_chunk = lax.rem(me, relays)
    quarter = lax.rem(me, quarters)
    my_rows = pl.multiple_of(quarter * ROWS, ROWS)
    my_lanes = pl.multiple_of((my_chunk // quarters) * LANES, LANES)
    count = n_dom * n_blk * faces * face_len
    share = w_cpl.shape[1] // n_blk
    span = w_inv.shape[0]
    width = subs * share
    all_peers = [(k - 1, lax.rem(me + k, n_dom)) for k in range(1, n_dom)]
    group_peers = [(k - 1, group + lax.rem(my_chunk + k, relays)) for k in range(1, relays)]
    near = (me // quarters) * quarters
    near_peers = [(k - 1, near + lax.rem(quarter + k, quarters)) for k in range(1, quarters)]
    blk_peers = [(k - 1, lax.rem(my_blk + k, n_blk)) for k in range(1, n_blk)]
    nt = (((1,), (1,)), ((), ()))

    loads = [
        pltpu.make_async_copy(src, dst, load.at[i])
        for i, (src, dst) in enumerate((
            (res_hbm, res), (dirichlet, w_dir), (dir_hbm, dirp),
            (coupling, w_cpl), (dual, w_dual), (inverse, w_inv),
        ))
    ]
    for copy in loads:
        copy.start()

    barrier = pltpu.get_barrier_semaphore()
    for axis, peers in (("dom", all_peers), ("blk", blk_peers)):
        for _, peer in peers:
            pl.semaphore_signal(barrier, inc=1, device_id={axis: peer}, device_id_type=MESH)

    span_of = (total_faces, id_rows.shape[2])
    face = lax.broadcasted_iota(jnp.int32, span_of, 0)
    place = lax.broadcasted_iota(jnp.int32, span_of, 1) * fps
    lowest = jnp.full(span_of, n_dom * slot_count - 1, jnp.int32)
    highest = jnp.zeros(span_of, jnp.int32)
    for t in range(fps):
        match = id_rows[t] == face
        lowest = jnp.where(match, jnp.minimum(lowest, place + t), lowest)
        highest = jnp.where(match, jnp.maximum(highest, place + t), highest)
    wide_to = (total_faces, 128)
    table[0] = jnp.broadcast_to(jnp.min(lowest, axis=1, keepdims=True), wide_to)
    table[1] = jnp.broadcast_to(jnp.max(highest, axis=1, keepdims=True), wide_to)
    tables = [
        pltpu.make_async_copy(table.at[i], into, load.at[6 + i])
        for i, into in enumerate((first, second))
    ]
    for copy in tables:
        copy.start()

    def chunk_of(k):
        h, q = k // quarters, k % quarters
        return q * ROWS, slice(h * LANES, (h + 1) * LANES)

    def start(copies):
        for copy in copies:
            copy.start()
        return copies

    def finish(copies):
        for copy in copies:
            copy.wait()

    def to_relays(turn, out, into):
        chunks, wide_by = out.shape[:2]
        copies = start([
            remote(
                out.at[lax.rem(peer, chunks)], into.at[pl.ds(me * wide_by, wide_by)],
                send_x.at[turn, k], recv_x.at[turn, k], "dom", peer,
            )
            for k, peer in all_peers
        ])
        into[pl.ds(me * wide_by, wide_by)] = out[lax.rem(me, chunks)]
        return copies

    def to_group(turn, source, into, peers=group_peers, here=my_chunk):
        copies = start([
            remote(
                source(peer), into.at[here],
                send_x.at[turn, k], recv_x.at[turn, k], "dom", peer,
            )
            for k, peer in peers
        ])
        into[here] = source(me)[...]
        return copies

    def face_of(d, s):
        return face_ids[s % fps, 0, d * subs + s // fps]

    def sign_of(s):
        return face_sign[s % fps, 0, me * subs + s // fps].astype(F32)

    def hand_out(turn, values):
        for i in range(relays):
            for s in range(0, slot_count, 2):
                slot_out[turn, i, s // 2] = pack(
                    values[face_of(group + i, s)], values[face_of(group + i, s + 1)]
                )
        return to_group(
            turn + 4, lambda peer: slot_out.at[turn, lax.rem(peer, relays)], slot_in.at[turn]
        )

    def to_slots(turn):
        for s in range(0, slot_count, 2):
            for h in range(halves):
                pairs = [
                    unpack(slot_in[turn, h * quarters + q, s // 2]) for q in range(quarters)
                ]
                for i in range(2):
                    sub, t = divmod(s + i, fps)
                    value = jnp.concatenate([pair[i] for pair in pairs], axis=0) * sign_of(s + i)
                    at = t * face_len + h * LANES
                    slots[STREAMS + turn, sub, :, at:at + LANES] = value.astype(BF16)

    def pulled_slots(st):
        for s in range(0, slot_count, 2):
            pairs = [unpack(pull_in[st, q, s // 2]) for q in range(quarters)]
            for i in range(2):
                sub, t = divmod(s + i, fps)
                value = jnp.concatenate([pair[i] for pair in pairs], axis=0) * sign_of(s + i)
                slots[st, sub, :, t * face_len:(t + 1) * face_len] = value.astype(BF16)

    def product(turn, weights, sub, t):
        return jnp.dot(
            slots[turn, sub], weights[sub, :, t * face_len:(t + 1) * face_len],
            preferred_element_type=F32,
        )

    def put(turn, s, one, other):
        for k in range(relays):
            row, lanes = chunk_of(k)
            push_out[turn, k, s // 2] = pack(one[row:row + ROWS, lanes], other[row:row + ROWS, lanes])

    def spread(turn):
        for i in range(n_dom * half_slots):
            pushed[2 * i], pushed[2 * i + 1] = unpack(push_in[turn, i])

    def face_sum(f):
        return pushed[first[f, 0]] + pushed[second[f, 0]]

    def reduce_start(turn, tile, axis, peers, into):
        part[turn] = tile
        here = lax.axis_index(axis)
        copies = start([
            remote(
                part.at[turn], into.at[here], send_s.at[turn, k], recv_s.at[turn, k], axis, peer
            )
            for k, peer in peers
        ])
        into[here] = tile
        return copies

    def reduce_end(copies, into, base, number):
        finish(copies)
        total = into[base]
        for i in range(1, number):
            total = total + into[base + i]
        return total

    loads[0].wait()
    for st in range(STREAMS):
        for f in range(0, faces, 2):
            for q in range(quarters):
                rows = slice(st * stream + q * ROWS, st * stream + (q + 1) * ROWS)
                res_out[st, q, f // 2] = pack(res[f, rows], res[f + 1, rows])
    pl.semaphore_wait(barrier, n_dom + n_blk - 2)
    pulled = [to_relays(st, res_out.at[st], res_in.at[st]) for st in range(STREAMS)]

    for b in range(n_blk):
        row = [ids_ref[s:s + 1, b * share:(b + 1) * share] for s in range(subs)]
        ids[n_blk + b, 0:1] = jnp.concatenate(row, axis=1) - b * span
    id_copies = start([
        remote(
            ids.at[n_blk + peer], ids.at[my_blk], send_t.at[4, k], recv_t.at[4, k], "blk", peer
        )
        for k, peer in blk_peers
    ])
    ids[my_blk] = ids[n_blk + my_blk]
    total = jnp.zeros((cases, face_len), F32)
    for f in range(faces):
        total += res[f] * res[f]
    square[...] = jnp.broadcast_to(lane_sum(total), (cases, 128))
    loads[2].wait()
    for st in range(STREAMS):
        for f in range(0, faces, 2):
            for k in range(relays):
                row, lanes = chunk_of(k)
                rows = slice(st * stream + row, st * stream + row + ROWS)
                dir_out[k, st * half_faces + f // 2] = pack(
                    dirp[f, rows, lanes], dirp[f + 1, rows, lanes]
                )

    handed = []
    for st in range(STREAMS):
        finish(pulled[st])
        for i in range(n_dom * half_faces):
            held[st, 2 * i], held[st, 2 * i + 1] = unpack(res_in[st, i])
        for i in range(quarters):
            for s in range(0, slot_count, 2):
                pull_out[st, i, s // 2] = pack(
                    held[st, face_of(near + i, s)], held[st, face_of(near + i, s + 1)]
                )
        handed.append(to_group(
            2 + st, lambda peer: pull_out.at[st, lax.rem(peer, quarters)], pull_in.at[st],
            near_peers, quarter,
        ))
    dir_copies = to_relays(6, dir_out, dir_in)
    finish(id_copies)
    finish(tables)
    for p in range(n_blk):
        rows = lax.broadcasted_iota(jnp.int32, (span, width), 0)
        hot[:, p * width:(p + 1) * width] = (rows == ids[p, 0:1, :]).astype(F32).astype(BF16)
    loads[1].wait()

    rho_copies, to_sum = [], []
    for st in range(STREAMS):
        finish(handed[st])
        pulled_slots(st)
        rho_part = jnp.zeros((stream, face_len), F32)
        for s in range(0, slot_count, 2):
            values = []
            for i in range(2):
                sub, t = divmod(s + i, fps)
                value = product(st, w_dir, sub, t)
                values.append(value * sign_of(s + i))
                rho_part += (
                    slots[st, sub, :, t * face_len:(t + 1) * face_len].astype(F32)
                    * value.astype(BF16).astype(F32)
                )
            put(st, s, *values)
        rows = slice(st * stream, (st + 1) * stream)
        tile = columns_tile((lane_sum(rho_part), square[rows, :1]))
        around = [jnp.zeros((st * stream, 128), F32)] if st else []
        after = jnp.zeros((128 - (st + 1) * stream, 128), F32)
        tile = jnp.transpose(jnp.concatenate(around + [tile, after], axis=0))[:8]
        rho_copies.append(reduce_start(st, tile, "dom", all_peers, dom_sums.at[st]))
        to_sum.append(to_relays(7 + st, push_out.at[st], push_in.at[st]))

    pad = jnp.ones((1, 128 - cases), F32)
    rho_prev = jnp.concatenate([rho_ref[...].reshape(1, cases), pad], axis=1)
    rho_now = jnp.zeros((1, 128), F32)
    square_sum = jnp.zeros((1, 128), F32)
    beta_row = jnp.zeros((1, 128), F32)
    for st in range(STREAMS):
        tile = reduce_end(rho_copies[st], dom_sums.at[st], 0, n_dom)
        copies = reduce_start(2 + st, tile, "blk", blk_peers, blk_sums.at[st])
        finish(to_sum[st])
        spread(st)
        if st == 0:
            finish(dir_copies)
        tile = reduce_end(copies, blk_sums.at[st], 0, n_blk)
        rho_now += tile[0:1] / count
        square_sum += tile[1:2]
        row = tile[0:1] / count / rho_prev
        beta_row += row
        column = as_column(row, cases)[st * stream:(st + 1) * stream]
        beta_wide[st] = jnp.broadcast_to(column, (stream, 128))
        beta = beta_wide[st, pl.ds(my_rows, ROWS), :]
        for owner in range(n_dom):
            for i in range(half_faces):
                f = owner * faces + 2 * i
                values = face_sum(f), face_sum(f + 1)
                at = st * half_faces + i
                precond_out[owner, at] = pack(*values)
                before = unpack(dir_in[owner * STREAMS * half_faces + at])
                direction[st, f] = values[0] + beta * before[0]
                direction[st, f + 1] = values[1] + beta * before[1]
        handed[st] = hand_out(st, direction.at[st])
    to_owners = to_group(9, lambda peer: precond_out.at[peer], precond_in)
    for i in (3, 4, 5):
        loads[i].wait()

    def blk_exchange(turn, out, into):
        copies = start([
            remote(out.at[peer], into.at[my_blk], send_t.at[turn, k], recv_t.at[turn, k], "blk", peer)
            for k, peer in blk_peers
        ])
        into[my_blk] = out[my_blk]
        return copies

    def terms(st):
        found = [
            lax.dot_general(slots[2 + st, s], w_cpl[s], nt, preferred_element_type=F32)
            for s in range(subs)
        ]
        for b in range(n_blk):
            terms_out[st, b] = jnp.concatenate(
                [value[:, b * share:(b + 1) * share] for value in found], axis=1
            ).astype(BF16)
        return blk_exchange(st, terms_out.at[st], terms_in.at[st])

    def dual_products(st):
        for s in range(slot_count):
            sub, t = divmod(s, fps)
            products[st, s] = product(2 + st, w_dual, sub, t)

    def solve(st):
        together = jnp.concatenate([terms_in[st, p].astype(F32) for p in range(n_blk)], axis=1)
        rhs = lax.dot_general(together.astype(BF16), hot[...], nt, preferred_element_type=F32)
        solved = jnp.dot(rhs.astype(BF16), w_inv[...], preferred_element_type=F32).astype(BF16)
        picked = jnp.dot(solved, hot[...], preferred_element_type=F32)
        for p in range(n_blk):
            picks_out[st, p] = picked[:, p * width:(p + 1) * width].astype(BF16)
        return blk_exchange(2 + st, picks_out.at[st], picks_in.at[st])

    def rows_out(st):
        for sub in range(subs):
            picked = jnp.concatenate([
                picks_in[st, b].astype(F32)[:, sub * share:(sub + 1) * share] for b in range(n_blk)
            ], axis=1).astype(BF16)
            for t in range(0, fps, 2):
                s = sub * fps + t
                put(2 + st, s, *[
                    (products[st, s + i] + jnp.dot(
                        picked, w_cpl[sub, :, (t + i) * face_len:(t + i + 1) * face_len],
                        preferred_element_type=F32,
                    )) * sign_of(s + i)
                    for i in range(2)
                ])
        return to_relays(10 + st, push_out.at[2 + st], push_in.at[2 + st])

    finish(handed[0])
    to_slots(0)
    first_terms = terms(0)
    dual_products(0)
    finish(first_terms)
    first_picks = solve(0)
    finish(handed[1])
    to_slots(1)
    second_terms = terms(1)
    dual_products(1)
    finish(first_picks)
    to_sum[0] = rows_out(0)
    finish(second_terms)
    second_picks = solve(1)
    finish(second_picks)
    to_sum[1] = rows_out(1)
    wide[...] = jnp.zeros((128, 128), F32)
    finish(to_owners)

    images = []
    for st in range(STREAMS):
        finish(to_sum[st])
        spread(2 + st)
        curve = jnp.zeros((ROWS, LANES), F32)
        cross = jnp.zeros((ROWS, LANES), F32)
        norm = jnp.zeros((ROWS, LANES), F32)
        for owner in range(n_dom):
            for i in range(half_faces):
                f = owner * faces + 2 * i
                values = face_sum(f), face_sum(f + 1)
                image_out[st, owner, i] = pack(*values)
                for j, value in enumerate(values):
                    curve += direction[st, f + j] * value
                    cross += held[st, f + j, :, pl.ds(my_lanes, LANES)] * value
                    norm += value * value
        at = pl.multiple_of(st * stream + my_rows, ROWS)
        wide[pl.ds(at, ROWS), :] = columns_tile((lane_sum(curve), lane_sum(cross), lane_sum(norm)))
        if st == STREAMS - 1:
            tile = jnp.transpose(wide[...])[:8]
            copies = reduce_start(4, tile, "dom", group_peers, dom_sums.at[2])
        images.append(to_group(
            12 + st, lambda peer: image_out.at[st, peer], image_in.at[st]
        ))
    tile = reduce_end(copies, dom_sums.at[2], group, relays)
    copies = reduce_start(5, tile, "blk", blk_peers, blk_sums.at[2])
    tile = reduce_end(copies, blk_sums.at[2], 0, n_blk)
    alpha = rho_now / (tile[0:1] / count)
    new_sum = square_sum - 2.0 * alpha * tile[1:2] + alpha * alpha * tile[2:3]
    stats[0:1] = rho_now
    stats[1:2] = (new_sum / count) / (square_sum / count)
    stats[2:3] = alpha
    stats[3:4] = beta_row
    stats[4:8] = jnp.zeros((4, 128), F32)
    for copies in images:
        finish(copies)


def finish_kernel(
    lam, res, dirp, precond, image, stats, new_lam, new_res, new_dir, rho_now, reduction
):
    faces, cases, face_len = lam.shape
    stream = cases // STREAMS
    quarters = stream // ROWS
    table = stats[...]
    alpha = as_column(table[2:3], cases)
    beta = as_column(table[3:4], cases)
    for st in range(STREAMS):
        for k in range(precond.shape[0]):
            row = st * stream + (k % quarters) * ROWS
            rows = slice(row, row + ROWS)
            lanes = slice((k // quarters) * LANES, (k // quarters + 1) * LANES)
            for i in range(faces // 2):
                sums = unpack(precond[k, st * (faces // 2) + i])
                images = unpack(image[st, k, i])
                for j in range(2):
                    f = 2 * i + j
                    direction = sums[j] + beta[rows] * dirp[f, rows, lanes]
                    new_dir[f, rows, lanes] = direction
                    new_lam[f, rows, lanes] = lam[f, rows, lanes] + alpha[rows] * direction
                    new_res[f, rows, lanes] = res[f, rows, lanes] - alpha[rows] * images[j]
    rho_now[...] = table[0:1, :cases].reshape(cases)
    reduction[...] = table[1:2, :cases].reshape(cases)


def on_device(
    multipliers, residual, dir_prev, rho_prev, face_ids, face_sign,
    dual_blocks, dirichlet_blocks, coupling, corner_ids, coarse_inv,
):
    n_dom, n_blk = lax.axis_size("dom"), lax.axis_size("blk")
    _, faces, cases, face_len = multipliers.shape
    _, subs, local, _ = dual_blocks.shape
    fps = face_ids.shape[2]
    slot_count = subs * fps
    stream = cases // STREAMS
    quarters = stream // ROWS
    relays = quarters * (face_len // LANES)
    total = n_dom * faces
    ids = jnp.transpose(face_ids, (2, 0, 1))
    signs = jnp.transpose(face_sign, (2, 0, 1))
    span = coarse_inv.shape[2]
    corners = coupling.shape[2]
    width = subs * (corners // n_blk)
    half_faces, half_slots = faces // 2, slot_count // 2
    field = jax.ShapeDtypeStruct((faces, cases, face_len), F32)
    vmem = pl.BlockSpec(memory_space=pltpu.VMEM)
    smem = pl.BlockSpec(memory_space=pltpu.SMEM)
    hbm = pl.BlockSpec(memory_space=pl.ANY)
    dma = pltpu.SemaphoreType.DMA
    terms = pltpu.VMEM((STREAMS, n_blk, stream, width), BF16)
    chunk = (ROWS, LANES)
    image, precond, stats = pl.pallas_call(
        step_kernel,
        out_shape=(
            jax.ShapeDtypeStruct((STREAMS, relays, half_faces) + PAIR, BF16),
            jax.ShapeDtypeStruct((relays, STREAMS * half_faces) + PAIR, BF16),
            jax.ShapeDtypeStruct((8, 128), F32),
        ),
        in_specs=[smem] * 2 + [vmem] + [hbm] * 2 + [vmem] * 2 + [hbm] * 4,
        out_specs=(vmem,) * 3,
        scratch_shapes=[
            pltpu.VMEM((subs, local, local), BF16),
            pltpu.VMEM((subs, local, local), BF16),
            pltpu.VMEM((subs, corners, local), BF16),
            pltpu.VMEM((span, span), BF16),
            pltpu.VMEM((faces, cases, face_len), F32),
            pltpu.VMEM((faces, cases, face_len), F32),
            pltpu.VMEM((STREAMS, quarters, half_faces, 2 * ROWS, face_len), BF16),
            pltpu.VMEM((STREAMS, n_dom * half_faces, 2 * ROWS, face_len), BF16),
            pltpu.VMEM((relays, STREAMS * half_faces) + PAIR, BF16),
            pltpu.VMEM((n_dom * STREAMS * half_faces,) + PAIR, BF16),
            pltpu.VMEM((STREAMS, quarters, half_slots, 2 * ROWS, face_len), BF16),
            pltpu.VMEM((STREAMS, quarters, half_slots, 2 * ROWS, face_len), BF16),
            pltpu.VMEM((STREAMS, relays, half_slots) + PAIR, BF16),
            pltpu.VMEM((STREAMS, relays, half_slots) + PAIR, BF16),
            pltpu.VMEM((2 * STREAMS, relays, half_slots) + PAIR, BF16),
            pltpu.VMEM((2 * STREAMS, n_dom * half_slots) + PAIR, BF16),
            pltpu.VMEM((n_dom, STREAMS * half_faces) + PAIR, BF16),
            pltpu.VMEM((STREAMS, n_dom, half_faces) + PAIR, BF16),
            pltpu.VMEM((STREAMS, total, ROWS, face_len), F32),
            pltpu.VMEM((STREAMS, total) + chunk, F32),
            pltpu.VMEM((n_dom * slot_count,) + chunk, F32),
            pltpu.VMEM((2 * STREAMS, subs, stream, local), BF16),
            pltpu.VMEM((STREAMS, slot_count, stream, face_len), F32),
            pltpu.VMEM((cases, 128), F32),
            pltpu.VMEM((6, 8, 128), F32),
            pltpu.VMEM((3, n_dom, 8, 128), F32),
            pltpu.VMEM((3, n_blk, 8, 128), F32),
            pltpu.VMEM((128, 128), F32),
            pltpu.VMEM((STREAMS, stream, 128), F32),
            pltpu.VMEM((span, n_blk * width), BF16),
            pltpu.VMEM((2 * n_blk, 8, width), jnp.int32),
            terms, terms, terms, terms,
            pltpu.VMEM((2, total, 128), jnp.int32),
            pltpu.SMEM((total, 128), jnp.int32),
            pltpu.SMEM((total, 128), jnp.int32),
            dma((8,)),
            dma((14, n_dom - 1)), dma((14, n_dom - 1)),
            dma((6, max(n_dom, n_blk) - 1)), dma((6, max(n_dom, n_blk) - 1)),
            dma((5, n_blk - 1)), dma((5, n_blk - 1)),
        ],
        compiler_params=pltpu.CompilerParams(
            collective_id=0, has_side_effects=True, vmem_limit_bytes=60 << 20
        ),
    )(
        ids, signs, ids, residual[0], dir_prev[0], rho_prev, corner_ids[0],
        dirichlet_blocks[0], dual_blocks[0], coupling[0], coarse_inv[0, 0],
    )
    row = jax.ShapeDtypeStruct((cases,), F32)
    new_lam, new_res, new_dir, rho_now, reduction = pl.pallas_call(
        finish_kernel,
        out_shape=(field, field, field, row, row),
        in_specs=[vmem] * 6,
        out_specs=(vmem,) * 5,
    )(multipliers[0], residual[0], dir_prev[0], precond, image, stats)
    return new_lam[None], new_res[None], new_dir[None], rho_now, reduction


def solution(mesh):
    in_specs = (
        P("blk", "dom", None, None),
        P("blk", "dom", None, None),
        P("blk", "dom", None, None),
        P(),
        P("blk", None, None),
        P("blk", None, None),
        P("blk", "dom", None, None),
        P("blk", "dom", None, None),
        P("blk", "dom", None, None),
        P("blk", "dom", None),
        P("dom", "blk", None, None),
    )
    out_specs = (
        P("blk", "dom", None, None),
        P("blk", "dom", None, None),
        P("blk", "dom", None, None),
        P(),
        P(),
    )
    return jax.shard_map(
        on_device, mesh=mesh, in_specs=in_specs, out_specs=out_specs, check_vma=False
    )
```

```python
import jax
import jax.numpy as jnp
from jax import lax
from jax.experimental import pallas as pl
from jax.experimental.pallas import tpu as pltpu
from jax.sharding import PartitionSpec as P

MESH = pl.DeviceIdType.MESH
F32, BF16 = jnp.float32, jnp.bfloat16
STREAMS = 2
ROWS, LANES = 8, 128
PAIR = (2 * ROWS, LANES)


def remote(src, dst, send, recv, axis, peer):
    return pltpu.make_async_remote_copy(
        src_ref=src, dst_ref=dst, send_sem=send, recv_sem=recv,
        device_id={axis: peer}, device_id_type=MESH,
    )


def pack(one, other):
    return jnp.concatenate([one, other], axis=0).astype(BF16)


def unpack(pair):
    pair = pair.astype(F32)
    return pair[:ROWS], pair[ROWS:]


def lane_sum(value):
    return jnp.sum(value, axis=1, keepdims=True)


def as_column(row, cases):
    tile = jnp.concatenate([row, jnp.zeros((127, row.shape[1]), F32)], axis=0)
    return jnp.transpose(tile)[:cases, :1]


def columns_tile(columns):
    rows = columns[0].shape[0]
    place = lax.broadcasted_iota(jnp.int32, (rows, 128), 1)
    tile = jnp.zeros((rows, 128), F32)
    for i, column in enumerate(columns):
        tile = jnp.where(place == i, column, tile)
    return tile


def step_kernel(
    face_ids, face_sign,
    id_rows, res_hbm, dir_hbm, rho_ref, ids_ref,
    dirichlet, dual, coupling, inverse,
    image_in, precond_in, stats,
    w_dir, w_dual, w_cpl, w_inv, res, dirp,
    res_out, res_in, dir_out, dir_in,
    pull_out, pull_in, slot_out, slot_in, push_out, push_in, precond_out, image_out,
    held, direction, pushed, slots, products, square,
    part, dom_sums, blk_sums, wide, beta_wide, hot, ids,
    terms_out, terms_in, picks_out, picks_in,
    table, first, second, load, send_x, recv_x, send_s, recv_s, send_t, recv_t,
):
    n_dom, n_blk = lax.axis_size("dom"), lax.axis_size("blk")
    me, my_blk = lax.axis_index("dom"), lax.axis_index("blk")
    faces, cases, face_len = res.shape
    subs = slots.shape[1]
    local = slots.shape[3]
    fps = local // face_len
    slot_count = subs * fps
    half_faces, half_slots = faces // 2, slot_count // 2
    total_faces = n_dom * faces
    stream = cases // STREAMS
    halves = face_len // LANES
    quarters = stream // ROWS
    relays = quarters * halves
    group = (me // relays) * relays
    my_chunk = lax.rem(me, relays)
    quarter = lax.rem(me, quarters)
    my_rows = pl.multiple_of(quarter * ROWS, ROWS)
    my_lanes = pl.multiple_of((my_chunk // quarters) * LANES, LANES)
    count = n_dom * n_blk * faces * face_len
    share = w_cpl.shape[1] // n_blk
    span = w_inv.shape[0]
    width = subs * share
    all_peers = [(k - 1, lax.rem(me + k, n_dom)) for k in range(n_dom - 1, 0, -1)]
    group_peers = [
        (k - 1, group + lax.rem(my_chunk + k, relays)) for k in range(relays - 1, 0, -1)
    ]
    near = (me // quarters) * quarters
    near_peers = [(k - 1, near + lax.rem(quarter + k, quarters)) for k in range(1, quarters)]
    blk_peers = [(k - 1, lax.rem(my_blk + k, n_blk)) for k in range(1, n_blk)]
    nt = (((1,), (1,)), ((), ()))

    loads = [
        pltpu.make_async_copy(src, dst, load.at[i])
        for i, (src, dst) in enumerate((
            (res_hbm, res), (dirichlet, w_dir), (dir_hbm, dirp),
            (coupling, w_cpl), (dual, w_dual), (inverse, w_inv),
        ))
    ]
    for copy in loads:
        copy.start()

    barrier = pltpu.get_barrier_semaphore()
    for axis, peers in (("dom", all_peers), ("blk", blk_peers)):
        for _, peer in peers:
            pl.semaphore_signal(barrier, inc=1, device_id={axis: peer}, device_id_type=MESH)

    span_of = (total_faces, id_rows.shape[2])
    face = lax.broadcasted_iota(jnp.int32, span_of, 0)
    place = lax.broadcasted_iota(jnp.int32, span_of, 1) * fps
    lowest = jnp.full(span_of, n_dom * slot_count - 1, jnp.int32)
    highest = jnp.zeros(span_of, jnp.int32)
    for t in range(fps):
        match = id_rows[t] == face
        lowest = jnp.where(match, jnp.minimum(lowest, place + t), lowest)
        highest = jnp.where(match, jnp.maximum(highest, place + t), highest)
    wide_to = (total_faces, 128)
    table[0] = jnp.broadcast_to(jnp.min(lowest, axis=1, keepdims=True), wide_to)
    table[1] = jnp.broadcast_to(jnp.max(highest, axis=1, keepdims=True), wide_to)
    tables = [
        pltpu.make_async_copy(table.at[i], into, load.at[6 + i])
        for i, into in enumerate((first, second))
    ]
    for copy in tables:
        copy.start()

    def chunk_of(k):
        h, q = k // quarters, k % quarters
        return q * ROWS, slice(h * LANES, (h + 1) * LANES)

    def start(copies):
        for copy in copies:
            copy.start()
        return copies

    def finish(copies):
        for copy in copies:
            copy.wait()

    def to_relays(turn, out, into):
        chunks, wide_by = out.shape[:2]
        copies = start([
            remote(
                out.at[lax.rem(peer, chunks)], into.at[pl.ds(me * wide_by, wide_by)],
                send_x.at[turn, k], recv_x.at[turn, k], "dom", peer,
            )
            for k, peer in all_peers
        ])
        into[pl.ds(me * wide_by, wide_by)] = out[lax.rem(me, chunks)]
        return copies

    def to_group(turn, source, into, peers=group_peers, here=my_chunk):
        copies = start([
            remote(
                source(peer), into.at[here],
                send_x.at[turn, k], recv_x.at[turn, k], "dom", peer,
            )
            for k, peer in peers
        ])
        into[here] = source(me)[...]
        return copies

    def face_of(d, s):
        return face_ids[s % fps, 0, d * subs + s // fps]

    def sign_of(s):
        return face_sign[s % fps, 0, me * subs + s // fps].astype(F32)

    def hand_out(turn, values):
        for i in range(relays):
            for s in range(0, slot_count, 2):
                slot_out[turn, i, s // 2] = pack(
                    values[face_of(group + i, s)], values[face_of(group + i, s + 1)]
                )
        return to_group(
            turn + 4, lambda peer: slot_out.at[turn, lax.rem(peer, relays)], slot_in.at[turn]
        )

    def to_slots(turn):
        for s in range(0, slot_count, 2):
            for h in range(halves):
                pairs = [
                    unpack(slot_in[turn, h * quarters + q, s // 2]) for q in range(quarters)
                ]
                for i in range(2):
                    sub, t = divmod(s + i, fps)
                    value = jnp.concatenate([pair[i] for pair in pairs], axis=0) * sign_of(s + i)
                    at = t * face_len + h * LANES
                    slots[STREAMS + turn, sub, :, at:at + LANES] = value.astype(BF16)

    def pulled_slots(st):
        for s in range(0, slot_count, 2):
            pairs = [unpack(pull_in[st, q, s // 2]) for q in range(quarters)]
            for i in range(2):
                sub, t = divmod(s + i, fps)
                value = jnp.concatenate([pair[i] for pair in pairs], axis=0) * sign_of(s + i)
                slots[st, sub, :, t * face_len:(t + 1) * face_len] = value.astype(BF16)

    def product(turn, weights, sub, t):
        return jnp.dot(
            slots[turn, sub], weights[sub, :, t * face_len:(t + 1) * face_len],
            preferred_element_type=F32,
        )

    def put(turn, s, one, other):
        for k in range(relays):
            row, lanes = chunk_of(k)
            push_out[turn, k, s // 2] = pack(one[row:row + ROWS, lanes], other[row:row + ROWS, lanes])

    def spread(turn):
        for i in range(n_dom * half_slots):
            pushed[2 * i], pushed[2 * i + 1] = unpack(push_in[turn, i])

    def face_sum(f):
        return pushed[first[f, 0]] + pushed[second[f, 0]]

    def reduce_start(turn, tile, axis, peers, into):
        part[turn] = tile
        here = lax.axis_index(axis)
        copies = start([
            remote(
                part.at[turn], into.at[here], send_s.at[turn, k], recv_s.at[turn, k], axis, peer
            )
            for k, peer in peers
        ])
        into[here] = tile
        return copies

    def reduce_end(copies, into, base, number):
        finish(copies)
        total = into[base]
        for i in range(1, number):
            total = total + into[base + i]
        return total

    loads[0].wait()
    for st in range(STREAMS):
        for f in range(0, faces, 2):
            for q in range(quarters):
                rows = slice(st * stream + q * ROWS, st * stream + (q + 1) * ROWS)
                res_out[st, q, f // 2] = pack(res[f, rows], res[f + 1, rows])
    pl.semaphore_wait(barrier, n_dom + n_blk - 2)
    pulled = [to_relays(st, res_out.at[st], res_in.at[st]) for st in range(STREAMS)]

    for b in range(n_blk):
        row = [ids_ref[s:s + 1, b * share:(b + 1) * share] for s in range(subs)]
        ids[n_blk + b, 0:1] = jnp.concatenate(row, axis=1) - b * span
    id_copies = start([
        remote(
            ids.at[n_blk + peer], ids.at[my_blk], send_t.at[4, k], recv_t.at[4, k], "blk", peer
        )
        for k, peer in blk_peers
    ])
    ids[my_blk] = ids[n_blk + my_blk]
    total = jnp.zeros((cases, face_len), F32)
    for f in range(faces):
        total += res[f] * res[f]
    square[...] = jnp.broadcast_to(lane_sum(total), (cases, 128))
    loads[2].wait()
    for st in range(STREAMS):
        for f in range(0, faces, 2):
            for k in range(relays):
                row, lanes = chunk_of(k)
                rows = slice(st * stream + row, st * stream + row + ROWS)
                dir_out[k, st * half_faces + f // 2] = pack(
                    dirp[f, rows, lanes], dirp[f + 1, rows, lanes]
                )

    handed = []
    for st in range(STREAMS):
        finish(pulled[st])
        for i in range(n_dom * half_faces):
            held[st, 2 * i], held[st, 2 * i + 1] = unpack(res_in[st, i])
        for i in range(quarters):
            for s in range(0, slot_count, 2):
                pull_out[st, i, s // 2] = pack(
                    held[st, face_of(near + i, s)], held[st, face_of(near + i, s + 1)]
                )
        handed.append(to_group(
            2 + st, lambda peer: pull_out.at[st, lax.rem(peer, quarters)], pull_in.at[st],
            near_peers, quarter,
        ))
    dir_copies = to_relays(6, dir_out, dir_in)
    finish(id_copies)
    finish(tables)
    for p in range(n_blk):
        rows = lax.broadcasted_iota(jnp.int32, (span, width), 0)
        hot[:, p * width:(p + 1) * width] = (rows == ids[p, 0:1, :]).astype(F32).astype(BF16)
    loads[1].wait()

    rho_copies, to_sum = [], []
    for st in range(STREAMS):
        finish(handed[st])
        pulled_slots(st)
        rho_part = jnp.zeros((stream, face_len), F32)
        for s in range(0, slot_count, 2):
            values = []
            for i in range(2):
                sub, t = divmod(s + i, fps)
                value = product(st, w_dir, sub, t)
                values.append(value * sign_of(s + i))
                rho_part += (
                    slots[st, sub, :, t * face_len:(t + 1) * face_len].astype(F32)
                    * value.astype(BF16).astype(F32)
                )
            put(st, s, *values)
        rows = slice(st * stream, (st + 1) * stream)
        tile = columns_tile((lane_sum(rho_part), square[rows, :1]))
        around = [jnp.zeros((st * stream, 128), F32)] if st else []
        after = jnp.zeros((128 - (st + 1) * stream, 128), F32)
        tile = jnp.transpose(jnp.concatenate(around + [tile, after], axis=0))[:8]
        rho_copies.append(reduce_start(st, tile, "dom", all_peers, dom_sums.at[st]))
        to_sum.append(to_relays(7 + st, push_out.at[st], push_in.at[st]))

    pad = jnp.ones((1, 128 - cases), F32)
    rho_prev = jnp.concatenate([rho_ref[...].reshape(1, cases), pad], axis=1)
    rho_now = jnp.zeros((1, 128), F32)
    square_sum = jnp.zeros((1, 128), F32)
    beta_row = jnp.zeros((1, 128), F32)
    for st in range(STREAMS):
        tile = reduce_end(rho_copies[st], dom_sums.at[st], 0, n_dom)
        copies = reduce_start(2 + st, tile, "blk", blk_peers, blk_sums.at[st])
        finish(to_sum[st])
        spread(st)
        if st == 0:
            finish(dir_copies)
        tile = reduce_end(copies, blk_sums.at[st], 0, n_blk)
        rho_now += tile[0:1] / count
        square_sum += tile[1:2]
        row = tile[0:1] / count / rho_prev
        beta_row += row
        column = as_column(row, cases)[st * stream:(st + 1) * stream]
        beta_wide[st] = jnp.broadcast_to(column, (stream, 128))
        beta = beta_wide[st, pl.ds(my_rows, ROWS), :]
        for owner in range(n_dom):
            for i in range(half_faces):
                f = owner * faces + 2 * i
                values = face_sum(f), face_sum(f + 1)
                at = st * half_faces + i
                precond_out[owner, at] = pack(*values)
                before = unpack(dir_in[owner * STREAMS * half_faces + at])
                direction[st, f] = values[0] + beta * before[0]
                direction[st, f + 1] = values[1] + beta * before[1]
        handed[st] = hand_out(st, direction.at[st])
    to_owners = to_group(9, lambda peer: precond_out.at[peer], precond_in)
    for i in (3, 4, 5):
        loads[i].wait()

    def blk_exchange(turn, out, into):
        copies = start([
            remote(out.at[peer], into.at[my_blk], send_t.at[turn, k], recv_t.at[turn, k], "blk", peer)
            for k, peer in blk_peers
        ])
        into[my_blk] = out[my_blk]
        return copies

    def terms(st):
        found = [
            lax.dot_general(slots[2 + st, s], w_cpl[s], nt, preferred_element_type=F32)
            for s in range(subs)
        ]
        for b in range(n_blk):
            terms_out[st, b] = jnp.concatenate(
                [value[:, b * share:(b + 1) * share] for value in found], axis=1
            ).astype(BF16)
        return blk_exchange(st, terms_out.at[st], terms_in.at[st])

    def dual_products(st):
        for s in range(slot_count):
            sub, t = divmod(s, fps)
            products[st, s] = product(2 + st, w_dual, sub, t)

    def solve(st):
        together = jnp.concatenate([terms_in[st, p].astype(F32) for p in range(n_blk)], axis=1)
        rhs = lax.dot_general(together.astype(BF16), hot[...], nt, preferred_element_type=F32)
        solved = jnp.dot(rhs.astype(BF16), w_inv[...], preferred_element_type=F32).astype(BF16)
        picked = jnp.dot(solved, hot[...], preferred_element_type=F32)
        for p in range(n_blk):
            picks_out[st, p] = picked[:, p * width:(p + 1) * width].astype(BF16)
        return blk_exchange(2 + st, picks_out.at[st], picks_in.at[st])

    def rows_out(st):
        for sub in range(subs):
            picked = jnp.concatenate([
                picks_in[st, b].astype(F32)[:, sub * share:(sub + 1) * share] for b in range(n_blk)
            ], axis=1).astype(BF16)
            for t in range(0, fps, 2):
                s = sub * fps + t
                put(2 + st, s, *[
                    (products[st, s + i] + jnp.dot(
                        picked, w_cpl[sub, :, (t + i) * face_len:(t + i + 1) * face_len],
                        preferred_element_type=F32,
                    )) * sign_of(s + i)
                    for i in range(2)
                ])
        return to_relays(10 + st, push_out.at[2 + st], push_in.at[2 + st])

    finish(handed[0])
    to_slots(0)
    first_terms = terms(0)
    dual_products(0)
    finish(first_terms)
    first_picks = solve(0)
    finish(handed[1])
    to_slots(1)
    second_terms = terms(1)
    dual_products(1)
    finish(first_picks)
    to_sum[0] = rows_out(0)
    finish(second_terms)
    second_picks = solve(1)
    finish(second_picks)
    to_sum[1] = rows_out(1)
    wide[...] = jnp.zeros((128, 128), F32)

    images = []
    for st in range(STREAMS):
        finish(to_sum[st])
        spread(2 + st)
        curve = jnp.zeros((ROWS, LANES), F32)
        cross = jnp.zeros((ROWS, LANES), F32)
        norm = jnp.zeros((ROWS, LANES), F32)
        for owner in range(n_dom):
            for i in range(half_faces):
                f = owner * faces + 2 * i
                values = face_sum(f), face_sum(f + 1)
                image_out[st, owner, i] = pack(*values)
                for j, value in enumerate(values):
                    curve += direction[st, f + j] * value
                    cross += held[st, f + j, :, pl.ds(my_lanes, LANES)] * value
                    norm += value * value
        at = pl.multiple_of(st * stream + my_rows, ROWS)
        wide[pl.ds(at, ROWS), :] = columns_tile((lane_sum(curve), lane_sum(cross), lane_sum(norm)))
        if st == STREAMS - 1:
            tile = jnp.transpose(wide[...])[:8]
            copies = reduce_start(4, tile, "dom", group_peers, dom_sums.at[2])
        images.append(to_group(
            12 + st, lambda peer: image_out.at[st, peer], image_in.at[st]
        ))
    tile = reduce_end(copies, dom_sums.at[2], group, relays)
    copies = reduce_start(5, tile, "blk", blk_peers, blk_sums.at[2])
    tile = reduce_end(copies, blk_sums.at[2], 0, n_blk)
    alpha = rho_now / (tile[0:1] / count)
    new_sum = square_sum - 2.0 * alpha * tile[1:2] + alpha * alpha * tile[2:3]
    stats[0:1] = rho_now
    stats[1:2] = (new_sum / count) / (square_sum / count)
    stats[2:3] = alpha
    stats[3:4] = beta_row
    stats[4:8] = jnp.zeros((4, 128), F32)
    for copies in images:
        finish(copies)
    finish(to_owners)


def finish_kernel(
    lam, res, dirp, precond, image, stats, new_lam, new_res, new_dir, rho_now, reduction
):
    faces, cases, face_len = lam.shape
    stream = cases // STREAMS
    quarters = stream // ROWS
    table = stats[...]
    alpha = as_column(table[2:3], cases)
    beta = as_column(table[3:4], cases)
    for st in range(STREAMS):
        for k in range(precond.shape[0]):
            row = st * stream + (k % quarters) * ROWS
            rows = slice(row, row + ROWS)
            lanes = slice((k // quarters) * LANES, (k // quarters + 1) * LANES)
            for i in range(faces // 2):
                sums = unpack(precond[k, st * (faces // 2) + i])
                images = unpack(image[st, k, i])
                for j in range(2):
                    f = 2 * i + j
                    direction = sums[j] + beta[rows] * dirp[f, rows, lanes]
                    new_dir[f, rows, lanes] = direction
                    new_lam[f, rows, lanes] = lam[f, rows, lanes] + alpha[rows] * direction
                    new_res[f, rows, lanes] = res[f, rows, lanes] - alpha[rows] * images[j]
    rho_now[...] = table[0:1, :cases].reshape(cases)
    reduction[...] = table[1:2, :cases].reshape(cases)


def on_device(
    multipliers, residual, dir_prev, rho_prev, face_ids, face_sign,
    dual_blocks, dirichlet_blocks, coupling, corner_ids, coarse_inv,
):
    n_dom, n_blk = lax.axis_size("dom"), lax.axis_size("blk")
    _, faces, cases, face_len = multipliers.shape
    _, subs, local, _ = dual_blocks.shape
    fps = face_ids.shape[2]
    slot_count = subs * fps
    stream = cases // STREAMS
    quarters = stream // ROWS
    relays = quarters * (face_len // LANES)
    total = n_dom * faces
    ids = jnp.transpose(face_ids, (2, 0, 1))
    signs = jnp.transpose(face_sign, (2, 0, 1))
    span = coarse_inv.shape[2]
    corners = coupling.shape[2]
    width = subs * (corners // n_blk)
    half_faces, half_slots = faces // 2, slot_count // 2
    field = jax.ShapeDtypeStruct((faces, cases, face_len), F32)
    vmem = pl.BlockSpec(memory_space=pltpu.VMEM)
    smem = pl.BlockSpec(memory_space=pltpu.SMEM)
    hbm = pl.BlockSpec(memory_space=pl.ANY)
    dma = pltpu.SemaphoreType.DMA
    terms = pltpu.VMEM((STREAMS, n_blk, stream, width), BF16)
    chunk = (ROWS, LANES)
    image, precond, stats = pl.pallas_call(
        step_kernel,
        out_shape=(
            jax.ShapeDtypeStruct((STREAMS, relays, half_faces) + PAIR, BF16),
            jax.ShapeDtypeStruct((relays, STREAMS * half_faces) + PAIR, BF16),
            jax.ShapeDtypeStruct((8, 128), F32),
        ),
        in_specs=[smem] * 2 + [vmem] + [hbm] * 2 + [vmem] * 2 + [hbm] * 4,
        out_specs=(vmem,) * 3,
        scratch_shapes=[
            pltpu.VMEM((subs, local, local), BF16),
            pltpu.VMEM((subs, local, local), BF16),
            pltpu.VMEM((subs, corners, local), BF16),
            pltpu.VMEM((span, span), BF16),
            pltpu.VMEM((faces, cases, face_len), F32),
            pltpu.VMEM((faces, cases, face_len), F32),
            pltpu.VMEM((STREAMS, quarters, half_faces, 2 * ROWS, face_len), BF16),
            pltpu.VMEM((STREAMS, n_dom * half_faces, 2 * ROWS, face_len), BF16),
            pltpu.VMEM((relays, STREAMS * half_faces) + PAIR, BF16),
            pltpu.VMEM((n_dom * STREAMS * half_faces,) + PAIR, BF16),
            pltpu.VMEM((STREAMS, quarters, half_slots, 2 * ROWS, face_len), BF16),
            pltpu.VMEM((STREAMS, quarters, half_slots, 2 * ROWS, face_len), BF16),
            pltpu.VMEM((STREAMS, relays, half_slots) + PAIR, BF16),
            pltpu.VMEM((STREAMS, relays, half_slots) + PAIR, BF16),
            pltpu.VMEM((2 * STREAMS, relays, half_slots) + PAIR, BF16),
            pltpu.VMEM((2 * STREAMS, n_dom * half_slots) + PAIR, BF16),
            pltpu.VMEM((n_dom, STREAMS * half_faces) + PAIR, BF16),
            pltpu.VMEM((STREAMS, n_dom, half_faces) + PAIR, BF16),
            pltpu.VMEM((STREAMS, total, ROWS, face_len), F32),
            pltpu.VMEM((STREAMS, total) + chunk, F32),
            pltpu.VMEM((n_dom * slot_count,) + chunk, F32),
            pltpu.VMEM((2 * STREAMS, subs, stream, local), BF16),
            pltpu.VMEM((STREAMS, slot_count, stream, face_len), F32),
            pltpu.VMEM((cases, 128), F32),
            pltpu.VMEM((6, 8, 128), F32),
            pltpu.VMEM((3, n_dom, 8, 128), F32),
            pltpu.VMEM((3, n_blk, 8, 128), F32),
            pltpu.VMEM((128, 128), F32),
            pltpu.VMEM((STREAMS, stream, 128), F32),
            pltpu.VMEM((span, n_blk * width), BF16),
            pltpu.VMEM((2 * n_blk, 8, width), jnp.int32),
            terms, terms, terms, terms,
            pltpu.VMEM((2, total, 128), jnp.int32),
            pltpu.SMEM((total, 128), jnp.int32),
            pltpu.SMEM((total, 128), jnp.int32),
            dma((8,)),
            dma((14, n_dom - 1)), dma((14, n_dom - 1)),
            dma((6, max(n_dom, n_blk) - 1)), dma((6, max(n_dom, n_blk) - 1)),
            dma((5, n_blk - 1)), dma((5, n_blk - 1)),
        ],
        compiler_params=pltpu.CompilerParams(
            collective_id=0, has_side_effects=True, vmem_limit_bytes=60 << 20
        ),
    )(
        ids, signs, ids, residual[0], dir_prev[0], rho_prev, corner_ids[0],
        dirichlet_blocks[0], dual_blocks[0], coupling[0], coarse_inv[0, 0],
    )
    row = jax.ShapeDtypeStruct((cases,), F32)
    new_lam, new_res, new_dir, rho_now, reduction = pl.pallas_call(
        finish_kernel,
        out_shape=(field, field, field, row, row),
        in_specs=[vmem] * 6,
        out_specs=(vmem,) * 5,
    )(multipliers[0], residual[0], dir_prev[0], precond, image, stats)
    return new_lam[None], new_res[None], new_dir[None], rho_now, reduction


def solution(mesh):
    in_specs = (
        P("blk", "dom", None, None),
        P("blk", "dom", None, None),
        P("blk", "dom", None, None),
        P(),
        P("blk", None, None),
        P("blk", None, None),
        P("blk", "dom", None, None),
        P("blk", "dom", None, None),
        P("blk", "dom", None, None),
        P("blk", "dom", None),
        P("dom", "blk", None, None),
    )
    out_specs = (
        P("blk", "dom", None, None),
        P("blk", "dom", None, None),
        P("blk", "dom", None, None),
        P(),
        P(),
    )
    return jax.shard_map(
        on_device, mesh=mesh, in_specs=in_specs, out_specs=out_specs, check_vma=False
    )
```

```python
import jax
import jax.numpy as jnp
from jax import lax
from jax.experimental import pallas as pl
from jax.experimental.pallas import tpu as pltpu
from jax.sharding import PartitionSpec as P

MESH = pl.DeviceIdType.MESH
F32, BF16 = jnp.float32, jnp.bfloat16
STREAMS = 2
ROWS, LANES = 8, 128
PAIR = (2 * ROWS, LANES)


def remote(src, dst, send, recv, axis, peer):
    return pltpu.make_async_remote_copy(
        src_ref=src, dst_ref=dst, send_sem=send, recv_sem=recv,
        device_id={axis: peer}, device_id_type=MESH,
    )


def pack(one, other):
    return jnp.concatenate([one, other], axis=0).astype(BF16)


def unpack(pair):
    pair = pair.astype(F32)
    return pair[:ROWS], pair[ROWS:]


def lane_sum(value):
    return jnp.sum(value, axis=1, keepdims=True)


def as_column(row, cases):
    tile = jnp.concatenate([row, jnp.zeros((127, row.shape[1]), F32)], axis=0)
    return jnp.transpose(tile)[:cases, :1]


def columns_tile(columns):
    rows = columns[0].shape[0]
    place = lax.broadcasted_iota(jnp.int32, (rows, 128), 1)
    tile = jnp.zeros((rows, 128), F32)
    for i, column in enumerate(columns):
        tile = jnp.where(place == i, column, tile)
    return tile


def step_kernel(
    face_ids, face_sign,
    id_rows, res_hbm, dir_hbm, rho_ref, ids_ref,
    dirichlet, dual, coupling, inverse,
    image_in, precond_in, stats,
    w_dir, w_dual, w_cpl, w_inv, res, dirp,
    res_out, res_in, dir_out, dir_in,
    pull_out, pull_in, slot_out, slot_in, push_out, push_in, precond_out, image_out,
    held, direction, pushed, slots, products, square,
    part, dom_sums, blk_sums, wide, beta_wide, hot, ids,
    terms_out, terms_in, picks_out, picks_in,
    table, first, second, load, send_x, recv_x, send_s, recv_s, send_t, recv_t,
):
    n_dom, n_blk = lax.axis_size("dom"), lax.axis_size("blk")
    me, my_blk = lax.axis_index("dom"), lax.axis_index("blk")
    faces, cases, face_len = res.shape
    subs = slots.shape[1]
    local = slots.shape[3]
    fps = local // face_len
    slot_count = subs * fps
    half_faces, half_slots = faces // 2, slot_count // 2
    total_faces = n_dom * faces
    stream = cases // STREAMS
    halves = face_len // LANES
    quarters = stream // ROWS
    relays = quarters * halves
    group = (me // relays) * relays
    my_chunk = lax.rem(me, relays)
    quarter = lax.rem(me, quarters)
    my_rows = pl.multiple_of(quarter * ROWS, ROWS)
    my_lanes = pl.multiple_of((my_chunk // quarters) * LANES, LANES)
    count = n_dom * n_blk * faces * face_len
    share = w_cpl.shape[1] // n_blk
    span = w_inv.shape[0]
    width = subs * share
    all_peers = [(k - 1, lax.rem(me + k, n_dom)) for k in range(n_dom - 1, 0, -1)]
    group_peers = [
        (k - 1, group + lax.rem(my_chunk + k, relays)) for k in range(relays - 1, 0, -1)
    ]
    near = (me // quarters) * quarters
    near_peers = [(k - 1, near + lax.rem(quarter + k, quarters)) for k in range(1, quarters)]
    blk_peers = [(k - 1, lax.rem(my_blk + k, n_blk)) for k in range(1, n_blk)]
    nt = (((1,), (1,)), ((), ()))

    loads = [
        pltpu.make_async_copy(src, dst, load.at[i])
        for i, (src, dst) in enumerate((
            (res_hbm, res), (dirichlet, w_dir), (dir_hbm, dirp),
            (coupling, w_cpl), (dual, w_dual), (inverse, w_inv),
        ))
    ]
    for copy in loads:
        copy.start()

    barrier = pltpu.get_barrier_semaphore()
    for axis, peers in (("dom", all_peers), ("blk", blk_peers)):
        for _, peer in peers:
            pl.semaphore_signal(barrier, inc=1, device_id={axis: peer}, device_id_type=MESH)

    span_of = (total_faces, id_rows.shape[2])
    face = lax.broadcasted_iota(jnp.int32, span_of, 0)
    place = lax.broadcasted_iota(jnp.int32, span_of, 1) * fps
    lowest = jnp.full(span_of, n_dom * slot_count - 1, jnp.int32)
    highest = jnp.zeros(span_of, jnp.int32)
    for t in range(fps):
        match = id_rows[t] == face
        lowest = jnp.where(match, jnp.minimum(lowest, place + t), lowest)
        highest = jnp.where(match, jnp.maximum(highest, place + t), highest)
    wide_to = (total_faces, 128)
    table[0] = jnp.broadcast_to(jnp.min(lowest, axis=1, keepdims=True), wide_to)
    table[1] = jnp.broadcast_to(jnp.max(highest, axis=1, keepdims=True), wide_to)
    tables = [
        pltpu.make_async_copy(table.at[i], into, load.at[6 + i])
        for i, into in enumerate((first, second))
    ]
    for copy in tables:
        copy.start()

    def chunk_of(k):
        h, q = k // quarters, k % quarters
        return q * ROWS, slice(h * LANES, (h + 1) * LANES)

    def start(copies):
        for copy in copies:
            copy.start()
        return copies

    def finish(copies):
        for copy in copies:
            copy.wait()

    def to_relays(turn, out, into):
        chunks, wide_by = out.shape[:2]
        copies = start([
            remote(
                out.at[lax.rem(peer, chunks)], into.at[pl.ds(me * wide_by, wide_by)],
                send_x.at[turn, k], recv_x.at[turn, k], "dom", peer,
            )
            for k, peer in all_peers
        ])
        into[pl.ds(me * wide_by, wide_by)] = out[lax.rem(me, chunks)]
        return copies

    def to_group(turn, source, into, peers=group_peers, here=my_chunk):
        copies = start([
            remote(
                source(peer), into.at[here],
                send_x.at[turn, k], recv_x.at[turn, k], "dom", peer,
            )
            for k, peer in peers
        ])
        into[here] = source(me)[...]
        return copies

    def face_of(d, s):
        return face_ids[s % fps, 0, d * subs + s // fps]

    def sign_of(s):
        return face_sign[s % fps, 0, me * subs + s // fps].astype(F32)

    def hand_out(turn, values):
        for i in range(relays):
            for s in range(0, slot_count, 2):
                slot_out[turn, i, s // 2] = pack(
                    values[face_of(group + i, s)], values[face_of(group + i, s + 1)]
                )
        return to_group(
            turn + 4, lambda peer: slot_out.at[turn, lax.rem(peer, relays)], slot_in.at[turn]
        )

    def to_slots(turn):
        for s in range(0, slot_count, 2):
            for h in range(halves):
                pairs = [
                    unpack(slot_in[turn, h * quarters + q, s // 2]) for q in range(quarters)
                ]
                for i in range(2):
                    sub, t = divmod(s + i, fps)
                    value = jnp.concatenate([pair[i] for pair in pairs], axis=0) * sign_of(s + i)
                    at = t * face_len + h * LANES
                    slots[STREAMS + turn, sub, :, at:at + LANES] = value.astype(BF16)

    def pulled_slots(st):
        for s in range(0, slot_count, 2):
            pairs = [unpack(pull_in[st, q, s // 2]) for q in range(quarters)]
            for i in range(2):
                sub, t = divmod(s + i, fps)
                value = jnp.concatenate([pair[i] for pair in pairs], axis=0) * sign_of(s + i)
                slots[st, sub, :, t * face_len:(t + 1) * face_len] = value.astype(BF16)

    def product(turn, weights, sub, t):
        return jnp.dot(
            slots[turn, sub], weights[sub, :, t * face_len:(t + 1) * face_len],
            preferred_element_type=F32,
        )

    def put(turn, s, one, other):
        for k in range(relays):
            row, lanes = chunk_of(k)
            push_out[turn, k, s // 2] = pack(one[row:row + ROWS, lanes], other[row:row + ROWS, lanes])

    def spread(turn):
        for i in range(n_dom * half_slots):
            pushed[2 * i], pushed[2 * i + 1] = unpack(push_in[turn, i])

    def face_sum(f):
        return pushed[first[f, 0]] + pushed[second[f, 0]]

    def reduce_start(turn, tile, axis, peers, into):
        part[turn] = tile
        here = lax.axis_index(axis)
        copies = start([
            remote(
                part.at[turn], into.at[here], send_s.at[turn, k], recv_s.at[turn, k], axis, peer
            )
            for k, peer in peers
        ])
        into[here] = tile
        return copies

    def reduce_end(copies, into, base, number):
        finish(copies)
        total = into[base]
        for i in range(1, number):
            total = total + into[base + i]
        return total

    loads[0].wait()
    for st in range(STREAMS):
        for f in range(0, faces, 2):
            for q in range(quarters):
                rows = slice(st * stream + q * ROWS, st * stream + (q + 1) * ROWS)
                res_out[st, q, f // 2] = pack(res[f, rows], res[f + 1, rows])
    pl.semaphore_wait(barrier, n_dom + n_blk - 2)
    pulled = [to_relays(st, res_out.at[st], res_in.at[st]) for st in range(STREAMS)]

    for b in range(n_blk):
        row = [ids_ref[s:s + 1, b * share:(b + 1) * share] for s in range(subs)]
        ids[n_blk + b, 0:1] = jnp.concatenate(row, axis=1) - b * span
    id_copies = start([
        remote(
            ids.at[n_blk + peer], ids.at[my_blk], send_t.at[4, k], recv_t.at[4, k], "blk", peer
        )
        for k, peer in blk_peers
    ])
    ids[my_blk] = ids[n_blk + my_blk]
    total = jnp.zeros((cases, face_len), F32)
    for f in range(faces):
        total += res[f] * res[f]
    square[...] = jnp.broadcast_to(lane_sum(total), (cases, 128))
    loads[2].wait()
    for st in range(STREAMS):
        for f in range(0, faces, 2):
            for k in range(relays):
                row, lanes = chunk_of(k)
                rows = slice(st * stream + row, st * stream + row + ROWS)
                dir_out[k, st * half_faces + f // 2] = pack(
                    dirp[f, rows, lanes], dirp[f + 1, rows, lanes]
                )

    handed = []
    for st in range(STREAMS):
        finish(pulled[st])
        for i in range(n_dom * half_faces):
            held[st, 2 * i], held[st, 2 * i + 1] = unpack(res_in[st, i])
        for i in range(quarters):
            for s in range(0, slot_count, 2):
                pull_out[st, i, s // 2] = pack(
                    held[st, face_of(near + i, s)], held[st, face_of(near + i, s + 1)]
                )
        handed.append(to_group(
            2 + st, lambda peer: pull_out.at[st, lax.rem(peer, quarters)], pull_in.at[st],
            near_peers, quarter,
        ))
    dir_copies = to_relays(6, dir_out, dir_in)
    finish(id_copies)
    finish(tables)
    for p in range(n_blk):
        rows = lax.broadcasted_iota(jnp.int32, (span, width), 0)
        hot[:, p * width:(p + 1) * width] = (rows == ids[p, 0:1, :]).astype(F32).astype(BF16)
    loads[1].wait()

    rho_copies, to_sum = [], []
    for st in range(STREAMS):
        finish(handed[st])
        pulled_slots(st)
        rho_part = jnp.zeros((stream, face_len), F32)
        for s in range(0, slot_count, 2):
            values = []
            for i in range(2):
                sub, t = divmod(s + i, fps)
                value = product(st, w_dir, sub, t)
                values.append(value * sign_of(s + i))
                rho_part += (
                    slots[st, sub, :, t * face_len:(t + 1) * face_len].astype(F32)
                    * value.astype(BF16).astype(F32)
                )
            put(st, s, *values)
        rows = slice(st * stream, (st + 1) * stream)
        tile = columns_tile((lane_sum(rho_part), square[rows, :1]))
        around = [jnp.zeros((st * stream, 128), F32)] if st else []
        after = jnp.zeros((128 - (st + 1) * stream, 128), F32)
        tile = jnp.transpose(jnp.concatenate(around + [tile, after], axis=0))[:8]
        rho_copies.append(reduce_start(st, tile, "dom", all_peers, dom_sums.at[st]))
        to_sum.append(to_relays(7 + st, push_out.at[st], push_in.at[st]))

    pad = jnp.ones((1, 128 - cases), F32)
    rho_prev = jnp.concatenate([rho_ref[...].reshape(1, cases), pad], axis=1)
    rho_now = jnp.zeros((1, 128), F32)
    square_sum = jnp.zeros((1, 128), F32)
    beta_row = jnp.zeros((1, 128), F32)
    for st in range(STREAMS):
        tile = reduce_end(rho_copies[st], dom_sums.at[st], 0, n_dom)
        copies = reduce_start(2 + st, tile, "blk", blk_peers, blk_sums.at[st])
        finish(to_sum[st])
        spread(st)
        if st == 0:
            finish(dir_copies)
        tile = reduce_end(copies, blk_sums.at[st], 0, n_blk)
        rho_now += tile[0:1] / count
        square_sum += tile[1:2]
        row = tile[0:1] / count / rho_prev
        beta_row += row
        column = as_column(row, cases)[st * stream:(st + 1) * stream]
        beta_wide[st] = jnp.broadcast_to(column, (stream, 128))
        beta = beta_wide[st, pl.ds(my_rows, ROWS), :]
        for owner in range(n_dom):
            for i in range(half_faces):
                f = owner * faces + 2 * i
                values = face_sum(f), face_sum(f + 1)
                at = st * half_faces + i
                before = unpack(dir_in[owner * STREAMS * half_faces + at])
                direction[st, f] = values[0] + beta * before[0]
                direction[st, f + 1] = values[1] + beta * before[1]
        handed[st] = hand_out(st, direction.at[st])
        for owner in range(n_dom):
            for i in range(half_faces):
                f = owner * faces + 2 * i
                precond_out[owner, st * half_faces + i] = pack(face_sum(f), face_sum(f + 1))
    to_owners = to_group(9, lambda peer: precond_out.at[peer], precond_in)
    for i in (3, 4, 5):
        loads[i].wait()

    def blk_exchange(turn, out, into):
        copies = start([
            remote(out.at[peer], into.at[my_blk], send_t.at[turn, k], recv_t.at[turn, k], "blk", peer)
            for k, peer in blk_peers
        ])
        into[my_blk] = out[my_blk]
        return copies

    def terms(st):
        found = [
            lax.dot_general(slots[2 + st, s], w_cpl[s], nt, preferred_element_type=F32)
            for s in range(subs)
        ]
        for b in range(n_blk):
            terms_out[st, b] = jnp.concatenate(
                [value[:, b * share:(b + 1) * share] for value in found], axis=1
            ).astype(BF16)
        return blk_exchange(st, terms_out.at[st], terms_in.at[st])

    def dual_products(st):
        for s in range(slot_count):
            sub, t = divmod(s, fps)
            products[st, s] = product(2 + st, w_dual, sub, t)

    def solve(st):
        together = jnp.concatenate([terms_in[st, p].astype(F32) for p in range(n_blk)], axis=1)
        rhs = lax.dot_general(together.astype(BF16), hot[...], nt, preferred_element_type=F32)
        solved = jnp.dot(rhs.astype(BF16), w_inv[...], preferred_element_type=F32).astype(BF16)
        picked = jnp.dot(solved, hot[...], preferred_element_type=F32)
        for p in range(n_blk):
            picks_out[st, p] = picked[:, p * width:(p + 1) * width].astype(BF16)
        return blk_exchange(2 + st, picks_out.at[st], picks_in.at[st])

    def rows_out(st):
        for sub in range(subs):
            picked = jnp.concatenate([
                picks_in[st, b].astype(F32)[:, sub * share:(sub + 1) * share] for b in range(n_blk)
            ], axis=1).astype(BF16)
            for t in range(0, fps, 2):
                s = sub * fps + t
                put(2 + st, s, *[
                    (products[st, s + i] + jnp.dot(
                        picked, w_cpl[sub, :, (t + i) * face_len:(t + i + 1) * face_len],
                        preferred_element_type=F32,
                    )) * sign_of(s + i)
                    for i in range(2)
                ])
        return to_relays(10 + st, push_out.at[2 + st], push_in.at[2 + st])

    finish(handed[0])
    to_slots(0)
    first_terms = terms(0)
    dual_products(0)
    finish(first_terms)
    first_picks = solve(0)
    finish(handed[1])
    to_slots(1)
    second_terms = terms(1)
    dual_products(1)
    finish(first_picks)
    to_sum[0] = rows_out(0)
    finish(second_terms)
    second_picks = solve(1)
    finish(second_picks)
    to_sum[1] = rows_out(1)
    wide[...] = jnp.zeros((128, 128), F32)

    images = []
    for st in range(STREAMS):
        finish(to_sum[st])
        spread(2 + st)
        curve = jnp.zeros((ROWS, LANES), F32)
        cross = jnp.zeros((ROWS, LANES), F32)
        norm = jnp.zeros((ROWS, LANES), F32)
        for owner in range(n_dom):
            for i in range(half_faces):
                f = owner * faces + 2 * i
                values = face_sum(f), face_sum(f + 1)
                image_out[st, owner, i] = pack(*values)
                for j, value in enumerate(values):
                    curve += direction[st, f + j] * value
                    cross += held[st, f + j, :, pl.ds(my_lanes, LANES)] * value
                    norm += value * value
        at = pl.multiple_of(st * stream + my_rows, ROWS)
        wide[pl.ds(at, ROWS), :] = columns_tile((lane_sum(curve), lane_sum(cross), lane_sum(norm)))
        if st == STREAMS - 1:
            tile = jnp.transpose(wide[...])[:8]
            copies = reduce_start(4, tile, "dom", group_peers, dom_sums.at[2])
        images.append(to_group(
            12 + st, lambda peer: image_out.at[st, peer], image_in.at[st]
        ))
    tile = reduce_end(copies, dom_sums.at[2], group, relays)
    copies = reduce_start(5, tile, "blk", blk_peers, blk_sums.at[2])
    tile = reduce_end(copies, blk_sums.at[2], 0, n_blk)
    alpha = rho_now / (tile[0:1] / count)
    new_sum = square_sum - 2.0 * alpha * tile[1:2] + alpha * alpha * tile[2:3]
    stats[0:1] = rho_now
    stats[1:2] = (new_sum / count) / (square_sum / count)
    stats[2:3] = alpha
    stats[3:4] = beta_row
    stats[4:8] = jnp.zeros((4, 128), F32)
    for copies in images:
        finish(copies)
    finish(to_owners)


def finish_kernel(
    lam, res, dirp, precond, image, stats, new_lam, new_res, new_dir, rho_now, reduction
):
    faces, cases, face_len = lam.shape
    stream = cases // STREAMS
    quarters = stream // ROWS
    table = stats[...]
    alpha = as_column(table[2:3], cases)
    beta = as_column(table[3:4], cases)
    for st in range(STREAMS):
        for k in range(precond.shape[0]):
            row = st * stream + (k % quarters) * ROWS
            rows = slice(row, row + ROWS)
            lanes = slice((k // quarters) * LANES, (k // quarters + 1) * LANES)
            for i in range(faces // 2):
                sums = unpack(precond[k, st * (faces // 2) + i])
                images = unpack(image[st, k, i])
                for j in range(2):
                    f = 2 * i + j
                    direction = sums[j] + beta[rows] * dirp[f, rows, lanes]
                    new_dir[f, rows, lanes] = direction
                    new_lam[f, rows, lanes] = lam[f, rows, lanes] + alpha[rows] * direction
                    new_res[f, rows, lanes] = res[f, rows, lanes] - alpha[rows] * images[j]
    rho_now[...] = table[0:1, :cases].reshape(cases)
    reduction[...] = table[1:2, :cases].reshape(cases)


def on_device(
    multipliers, residual, dir_prev, rho_prev, face_ids, face_sign,
    dual_blocks, dirichlet_blocks, coupling, corner_ids, coarse_inv,
):
    n_dom, n_blk = lax.axis_size("dom"), lax.axis_size("blk")
    _, faces, cases, face_len = multipliers.shape
    _, subs, local, _ = dual_blocks.shape
    fps = face_ids.shape[2]
    slot_count = subs * fps
    stream = cases // STREAMS
    quarters = stream // ROWS
    relays = quarters * (face_len // LANES)
    total = n_dom * faces
    ids = jnp.transpose(face_ids, (2, 0, 1))
    signs = jnp.transpose(face_sign, (2, 0, 1))
    span = coarse_inv.shape[2]
    corners = coupling.shape[2]
    width = subs * (corners // n_blk)
    half_faces, half_slots = faces // 2, slot_count // 2
    field = jax.ShapeDtypeStruct((faces, cases, face_len), F32)
    vmem = pl.BlockSpec(memory_space=pltpu.VMEM)
    smem = pl.BlockSpec(memory_space=pltpu.SMEM)
    hbm = pl.BlockSpec(memory_space=pl.ANY)
    dma = pltpu.SemaphoreType.DMA
    terms = pltpu.VMEM((STREAMS, n_blk, stream, width), BF16)
    chunk = (ROWS, LANES)
    image, precond, stats = pl.pallas_call(
        step_kernel,
        out_shape=(
            jax.ShapeDtypeStruct((STREAMS, relays, half_faces) + PAIR, BF16),
            jax.ShapeDtypeStruct((relays, STREAMS * half_faces) + PAIR, BF16),
            jax.ShapeDtypeStruct((8, 128), F32),
        ),
        in_specs=[smem] * 2 + [vmem] + [hbm] * 2 + [vmem] * 2 + [hbm] * 4,
        out_specs=(vmem,) * 3,
        scratch_shapes=[
            pltpu.VMEM((subs, local, local), BF16),
            pltpu.VMEM((subs, local, local), BF16),
            pltpu.VMEM((subs, corners, local), BF16),
            pltpu.VMEM((span, span), BF16),
            pltpu.VMEM((faces, cases, face_len), F32),
            pltpu.VMEM((faces, cases, face_len), F32),
            pltpu.VMEM((STREAMS, quarters, half_faces, 2 * ROWS, face_len), BF16),
            pltpu.VMEM((STREAMS, n_dom * half_faces, 2 * ROWS, face_len), BF16),
            pltpu.VMEM((relays, STREAMS * half_faces) + PAIR, BF16),
            pltpu.VMEM((n_dom * STREAMS * half_faces,) + PAIR, BF16),
            pltpu.VMEM((STREAMS, quarters, half_slots, 2 * ROWS, face_len), BF16),
            pltpu.VMEM((STREAMS, quarters, half_slots, 2 * ROWS, face_len), BF16),
            pltpu.VMEM((STREAMS, relays, half_slots) + PAIR, BF16),
            pltpu.VMEM((STREAMS, relays, half_slots) + PAIR, BF16),
            pltpu.VMEM((2 * STREAMS, relays, half_slots) + PAIR, BF16),
            pltpu.VMEM((2 * STREAMS, n_dom * half_slots) + PAIR, BF16),
            pltpu.VMEM((n_dom, STREAMS * half_faces) + PAIR, BF16),
            pltpu.VMEM((STREAMS, n_dom, half_faces) + PAIR, BF16),
            pltpu.VMEM((STREAMS, total, ROWS, face_len), F32),
            pltpu.VMEM((STREAMS, total) + chunk, F32),
            pltpu.VMEM((n_dom * slot_count,) + chunk, F32),
            pltpu.VMEM((2 * STREAMS, subs, stream, local), BF16),
            pltpu.VMEM((STREAMS, slot_count, stream, face_len), F32),
            pltpu.VMEM((cases, 128), F32),
            pltpu.VMEM((6, 8, 128), F32),
            pltpu.VMEM((3, n_dom, 8, 128), F32),
            pltpu.VMEM((3, n_blk, 8, 128), F32),
            pltpu.VMEM((128, 128), F32),
            pltpu.VMEM((STREAMS, stream, 128), F32),
            pltpu.VMEM((span, n_blk * width), BF16),
            pltpu.VMEM((2 * n_blk, 8, width), jnp.int32),
            terms, terms, terms, terms,
            pltpu.VMEM((2, total, 128), jnp.int32),
            pltpu.SMEM((total, 128), jnp.int32),
            pltpu.SMEM((total, 128), jnp.int32),
            dma((8,)),
            dma((14, n_dom - 1)), dma((14, n_dom - 1)),
            dma((6, max(n_dom, n_blk) - 1)), dma((6, max(n_dom, n_blk) - 1)),
            dma((5, n_blk - 1)), dma((5, n_blk - 1)),
        ],
        compiler_params=pltpu.CompilerParams(
            collective_id=0, has_side_effects=True, vmem_limit_bytes=60 << 20
        ),
    )(
        ids, signs, ids, residual[0], dir_prev[0], rho_prev, corner_ids[0],
        dirichlet_blocks[0], dual_blocks[0], coupling[0], coarse_inv[0, 0],
    )
    row = jax.ShapeDtypeStruct((cases,), F32)
    new_lam, new_res, new_dir, rho_now, reduction = pl.pallas_call(
        finish_kernel,
        out_shape=(field, field, field, row, row),
        in_specs=[vmem] * 6,
        out_specs=(vmem,) * 5,
    )(multipliers[0], residual[0], dir_prev[0], precond, image, stats)
    return new_lam[None], new_res[None], new_dir[None], rho_now, reduction


def solution(mesh):
    in_specs = (
        P("blk", "dom", None, None),
        P("blk", "dom", None, None),
        P("blk", "dom", None, None),
        P(),
        P("blk", None, None),
        P("blk", None, None),
        P("blk", "dom", None, None),
        P("blk", "dom", None, None),
        P("blk", "dom", None, None),
        P("blk", "dom", None),
        P("dom", "blk", None, None),
    )
    out_specs = (
        P("blk", "dom", None, None),
        P("blk", "dom", None, None),
        P("blk", "dom", None, None),
        P(),
        P(),
    )
    return jax.shard_map(
        on_device, mesh=mesh, in_specs=in_specs, out_specs=out_specs, check_vma=False
    )
```
